256 devices in a mesh: grow: 16 (over z_lo, x), wide: 16 (over z_hi, y, core).
Axes of the slice: x: 4, y: 4, z: 8 (z_hi: 2, z_lo: 4; z = z_hi * 4 + z_lo), core: 2. Of those that a mesh axis runs over, the one named last changes fastest.
Arguments:
- fields: float32 [3, 256, 512, 128], P(None, 'grow', 'wide'), may hold values from -1 to 1
- melt_planes: float32 [3, 16, 512, 128], P(None, None, 'wide'), may hold values from -1 to 1
- slide_planes: int32 [8], replicated, may hold values from 0 to 8, as said below
Outputs:
- evolved: float32 [3, 256, 512, 128], P(None, 'grow', 'wide')
The draws below stay inside these ranges and needn't reach their ends.
Inputs may be any that keep to these rules, and one draw needn't show every extreme that they name: `slide_planes`: entries at even positions k are 0; at least one entry equals 8, and at most one other entry is nonzero.
All inputs are finite; a program needn't handle non-finite values.
Results may differ from the reference program's by a relative error of at most 0.0001.
Values sent between devices are 32-bit elements; how exact they have to be, the bound alone decides.
A program may use at most 64 MiB of HBM per device.

```python
import jax
import jax.numpy as jnp
from jax import lax

CX = 16
NZ = 128
SUBSTEPS = 8
NX = 256
NY = 512


def draw_slide_planes(key, part):
    base = jax.random.fold_in(key, 7)
    key_order, key_count = jax.random.split(base)
    ranking = jax.random.permutation(key_order, SUBSTEPS // 2)
    second_count = jax.random.randint(key_count, (), 0, CX // 2 + 1)
    counts = jnp.where(ranking == 0, CX // 2, jnp.where(ranking == 1, second_count, 0)).astype(jnp.int32)
    odd_slots = 2 * jnp.arange(SUBSTEPS // 2) + 1
    planes = jnp.zeros((SUBSTEPS,), jnp.int32).at[odd_slots].set(counts)
    return planes


def shard_levels(key, shape, cuts, low, high):
    loudness, own = 1.0, jax.random.fold_in(key, 6)
    for dim, parts in cuts:
        steps = jnp.exp(jax.random.uniform(jax.random.fold_in(own, dim), (parts,), jnp.float32, low / len(cuts), high / len(cuts)))
        loudness = loudness * jnp.repeat(steps, shape[dim] // parts).reshape([-1 if axis == dim else 1 for axis in range(len(shape))])
    return loudness


def setup_inputs(seed: int = 0) -> dict:
    key_list = jax.random.split(jax.random.key(seed), 4)
    return {
        "fields": jnp.clip(jax.random.uniform(key_list[0], (3, NX, NY, NZ), jnp.float32, -1.0, 1.0) * shard_levels(key_list[0], (3, NX, NY, NZ), ((1, 16), (2, 16)), -0.4, 0.0), -1.0, 1.0),
        "melt_planes": jnp.clip(jax.random.uniform(key_list[1], (3, CX, NY, NZ), jnp.float32, -1.0, 1.0) * shard_levels(key_list[1], (3, CX, NY, NZ), ((2, 16),), -0.4, 0.0), -1.0, 1.0),
        "slide_planes": draw_slide_planes(jax.random.fold_in(key_list[3], 71), 0),
    }


coef_phase = 0.15
coef_react = 0.3
coef_couple = 0.4
coef_solute = 1.5
coef_diff = 0.1
coef_heat = 0.16


def laplace(field):
    padded = jnp.pad(field, ((1, 1), (1, 1), (0, 0)))
    return (padded[2:, 1:-1] + padded[:-2, 1:-1] + padded[1:-1, 2:] + padded[1:-1, :-2]
            + jnp.roll(field, 1, 2) + jnp.roll(field, -1, 2) - 6.0 * field)


def advance(phase_now, solute, thermal):
    squared = 1.0 - phase_now * phase_now
    driving = (phase_now + coef_phase * laplace(phase_now)
               + coef_react * (phase_now - phase_now * phase_now * phase_now)
               - coef_couple * squared * squared * (thermal + coef_solute * solute))
    grown = jnp.tanh(driving)
    change = 0.5 * (grown - phase_now)
    solute_next = solute + coef_diff * laplace(solute) + change
    thermal_next = thermal + coef_heat * laplace(thermal) + change
    return grown, solute_next, thermal_next


def slide_field(field, melt_field, shift, cursor):
    doubled = jnp.concatenate([melt_field, melt_field], 0)
    entering = lax.dynamic_slice_in_dim(doubled, cursor, CX, 0)
    combined = jnp.concatenate([field, entering], 0)
    return lax.dynamic_slice_in_dim(combined, shift, NX, 0)


def reference(fields, melt_planes, slide_planes):
    phase_now, solute, thermal = fields[0], fields[1], fields[2]
    for substep in range(SUBSTEPS):
        phase_now, solute, thermal = advance(phase_now, solute, thermal)
        shift = slide_planes[substep].astype(jnp.int32)
        cursor = jnp.sum(slide_planes[:substep]).astype(jnp.int32)
        phase_now = slide_field(phase_now, melt_planes[0], shift, cursor)
        solute = slide_field(solute, melt_planes[1], shift, cursor)
        thermal = slide_field(thermal, melt_planes[2], shift, cursor)
    return jnp.stack([phase_now, solute, thermal])
```

```python
import functools

import jax
import jax.numpy as jnp
from jax import lax
from jax.experimental import pallas as pl
from jax.experimental.pallas import tpu as pltpu
from jax.sharding import PartitionSpec as P

MESH = pl.DeviceIdType.MESH
STEPS = 8
OWN = 16
FAR = 8
PLANES = OWN + OWN + FAR
COLS = 32
LO = 16
ROWS = 64
CHUNK = 2
NEAR_CHUNKS = OWN // CHUNK
FAR_CHUNKS = FAR // CHUNK
CHUNKS = NEAR_CHUNKS + FAR_CHUNKS
LAG = 2


def kernel(G, W, slide, fields, melt, out, lev, mbuf, cur, local_sem, x_send, x_recv, y_send, y_recv, m_send, m_recv):
    g = lax.axis_index("grow")
    w = lax.axis_index("wide")
    base = OWN * (G - g)
    has_left, has_right = w > 0, w < W - 1
    partners = (
        (g > 0, {"grow": g - 1}), (g < G - 1, {"grow": g + 1}),
        (g > 1, {"grow": g - 2}), (g < G - 2, {"grow": g + 2}),
        (has_left, {"wide": w - 1}), (has_right, {"wide": w + 1}),
    )
    barrier = pltpu.get_barrier_semaphore()
    count = jnp.int32(0)
    for there, device in partners:
        count = count + there.astype(jnp.int32)

        @pl.when(there)
        def _():
            pl.semaphore_signal(barrier, inc=1, device_id=device, device_id_type=MESH)

    own = pltpu.make_async_copy(fields, lev.at[0, :, pl.ds(0, OWN), pl.ds(LO, COLS), :], local_sem.at[0])
    own.start()
    melt_in = pltpu.make_async_copy(melt, mbuf.at[:, :, pl.ds(LO, COLS), :], local_sem.at[1])

    @pl.when(g >= G - 2)
    def _():
        melt_in.start()

    cursor = jnp.int32(0)
    cur[0] = cursor
    for k in range(STEPS):
        cursor = cursor + slide[k]
        cur[k + 1] = cursor

    zeros = jnp.zeros((8, 128), jnp.float32)
    for side_there, row in ((has_left, LO - 8), (has_right, LO + COLS)):

        @pl.when(jnp.logical_not(side_there))
        def _():
            @pl.loop(0, PLANES)
            def _(x):
                for f in range(3):
                    lev[0, f, x, pl.ds(row, 8), :] = zeros

            @pl.loop(0, OWN)
            def _(x):
                for f in range(3):
                    mbuf[f, x, pl.ds(row, 8), :] = zeros

    def zero_planes(first, last):
        @pl.loop(first, last)
        def _(x):
            for f in range(3):
                for k in range(6):
                    lev[0, f, x, pl.ds(LO - 8 + 8 * k, 8), :] = zeros

    @pl.when(g == G - 1)
    def _():
        zero_planes(OWN, PLANES)

    @pl.when(g == G - 2)
    def _():
        zero_planes(2 * OWN, PLANES)

    def x_copy(c):
        return pltpu.make_async_remote_copy(
            src_ref=fields.at[:, pl.ds(CHUNK * c, CHUNK)],
            dst_ref=lev.at[0, :, pl.ds(OWN + CHUNK * c, CHUNK), pl.ds(LO, COLS), :],
            send_sem=x_send.at[c], recv_sem=x_recv.at[c], device_id={"grow": g - 1}, device_id_type=MESH)

    def far_copy(c):
        return pltpu.make_async_remote_copy(
            src_ref=fields.at[:, pl.ds(CHUNK * c, CHUNK)],
            dst_ref=lev.at[0, :, pl.ds(2 * OWN + CHUNK * c, CHUNK), pl.ds(LO, COLS), :],
            send_sem=x_send.at[NEAR_CHUNKS + c], recv_sem=x_recv.at[NEAR_CHUNKS + c],
            device_id={"grow": g - 2}, device_id_type=MESH)

    def y_own(side):
        rows, to, there = ((0, LO + COLS, w - 1), (COLS - 8, LO - 8, w + 1))[side]
        return pltpu.make_async_remote_copy(
            src_ref=fields.at[:, :, pl.ds(rows, 8), :],
            dst_ref=lev.at[0, :, pl.ds(0, OWN), pl.ds(to, 8), :],
            send_sem=y_send.at[side, CHUNKS], recv_sem=y_recv.at[side, CHUNKS],
            device_id={"wide": there}, device_id_type=MESH)

    def y_melt(side):
        rows, to, there = ((0, LO + COLS, w - 1), (COLS - 8, LO - 8, w + 1))[side]
        return pltpu.make_async_remote_copy(
            src_ref=melt.at[:, :, pl.ds(rows, 8), :],
            dst_ref=mbuf.at[:, :, pl.ds(to, 8), :],
            send_sem=m_send.at[side], recv_sem=m_recv.at[side],
            device_id={"wide": there}, device_id_type=MESH)

    def y_copy(side, c):
        rows, to, there = ((LO, LO + COLS, w - 1), (LO + COLS - 8, LO - 8, w + 1))[side]
        x = OWN + CHUNK * c
        return pltpu.make_async_remote_copy(
            src_ref=lev.at[0, :, pl.ds(x, CHUNK), pl.ds(rows, 8), :],
            dst_ref=lev.at[0, :, pl.ds(x, CHUNK), pl.ds(to, 8), :],
            send_sem=y_send.at[side, c], recv_sem=y_recv.at[side, c],
            device_id={"wide": there}, device_id_type=MESH)

    sends = (has_left, has_right)
    receives = (has_right, has_left)

    pl.semaphore_wait(barrier, count)
    for side in (0, 1):
        @pl.when(sends[side])
        def _():
            y_own(side).start()

    @pl.when(g > 0)
    def _():
        @pl.loop(0, NEAR_CHUNKS)
        def _(c):
            x_copy(c).start()

    @pl.when(g > 1)
    def _():
        @pl.loop(0, FAR_CHUNKS)
        def _(c):
            far_copy(c).start()

    @pl.when(g >= G - 2)
    def _():
        for side in (0, 1):
            @pl.when(sends[side])
            def _():
                y_melt(side).start()

    def pair(t, x):
        for k in range(6):
            row = LO - 8 + 8 * k
            total, centre = [[], []], [[], []]
            for f in range(3):
                along = [lev[t, f, x + d, pl.ds(row, 8), :] for d in (-1, 0, 1, 2)]
                for q in range(2):
                    here = along[q + 1]
                    around = along[q] + along[q + 2]
                    around = around + lev[t, f, x + q, pl.ds(row - 1, 8), :] + lev[t, f, x + q, pl.ds(row + 1, 8), :]
                    around = around + (pltpu.roll(here, 1, 1) + pltpu.roll(here, 127, 1))
                    total[q].append(around)
                    centre[q].append(here)
            for q in range(2):
                p, s, h = centre[q]
                p2 = p * p
                rest = 1.0 - p2
                drive = p * (0.4 - 0.3 * p2) + 0.15 * total[q][0] - rest * rest * (0.4 * h + 0.6 * s)
                grown = jnp.tanh(drive)
                change = 0.5 * (grown - p)
                s = (0.4 * s + 0.1 * total[q][1]) + change
                h = (0.04 * h + 0.16 * total[q][2]) + change
                new = [grown, s, h]
                if k == 0:
                    new = [jnp.where(has_left, v, 0.0) for v in new]
                if k == 5:
                    new = [jnp.where(has_right, v, 0.0) for v in new]
                for f in range(3):
                    lev[t + 1, f, x + q, pl.ds(row, 8), :] = new[f]

    span = pl.ds(LO - 8, COLS + 16)

    def left_edge(t, x):
        @pl.when(jnp.logical_and(g == 0, x < OWN))
        def _():
            for q in range(2):
                keep = x + q >= cur[t + 1]
                for f in range(3):
                    lev[t + 1, f, x + q, span, :] = jnp.where(keep, lev[t + 1, f, x + q, span, :], 0.0)

    def right_edge(t, x):
        for q in range(2):
            @pl.when(x + q >= base)
            def _():
                plane = x + q - base
                inside = cur[t] > plane
                enters = cur[t + 1] > plane
                slot = jnp.minimum(plane, OWN - 1)
                for f in range(3):
                    fresh = jnp.where(enters, mbuf[f, slot, span, :], 0.0)
                    lev[t + 1, f, x + q, span, :] = jnp.where(inside, lev[t + 1, f, x + q, span, :], fresh)

    own.wait()
    for side in (0, 1):
        @pl.when(receives[side])
        def _():
            y_own(side).wait_recv()

    @pl.when(g >= G - 2)
    def _():
        melt_in.wait()
        for side in (0, 1):
            @pl.when(receives[side])
            def _():
                y_melt(side).wait_recv()

    @pl.loop(0, STEPS - 1)
    def _(t):
        @pl.loop(0, OWN // 2 - 1 - t)
        def _(i):
            x = t + 1 + 2 * i
            pair(t, x)
            left_edge(t, x)

    def pass_on(c):
        for side in (0, 1):
            @pl.when(sends[side])
            def _():
                y_copy(side, c).start()

    def edges_in(c):
        for side in (0, 1):
            @pl.when(receives[side])
            def _():
                y_copy(side, c).wait_recv()

    @pl.loop(0, NEAR_CHUNKS + LAG)
    def _(it):
        @pl.when(jnp.logical_and(it < NEAR_CHUNKS, g < G - 1))
        def _():
            x_copy(it).wait_recv()
            pass_on(it)

            @pl.when(jnp.logical_and(it % 2 == 1, g < G - 2))
            def _():
                far_copy(it // 2).wait_recv()
                pass_on(NEAR_CHUNKS + it // 2)

        @pl.when(it >= LAG)
        def _():
            c = it - LAG

            @pl.when(g < G - 1)
            def _():
                edges_in(c)

            @pl.loop(0, STEPS)
            def _(t):
                x = OWN + CHUNK * c - 1 - t
                pair(t, x)
                left_edge(t, x)
                right_edge(t, x)

    @pl.when(g < G - 2)
    def _():
        @pl.loop(NEAR_CHUNKS, CHUNKS)
        def _(c):
            edges_in(c)

    @pl.loop(0, STEPS)
    def _(t):
        @pl.loop(0, FAR // 2)
        def _(i):
            x = 2 * OWN - 1 - t + 2 * i
            pair(t, x)
            right_edge(t, x)

    shift = cur[STEPS]
    @pl.loop(0, OWN)
    def _(x):
        for f in range(3):
            out[f, x] = lev[STEPS, f, shift + x, pl.ds(LO, COLS), :]

    for side in (0, 1):
        @pl.when(sends[side])
        def _():
            y_own(side).wait_send()

            @pl.when(g >= G - 2)
            def _():
                y_melt(side).wait_send()

            @pl.when(g < G - 1)
            def _():
                @pl.loop(0, NEAR_CHUNKS)
                def _(c):
                    y_copy(side, c).wait_send()

            @pl.when(g < G - 2)
            def _():
                @pl.loop(NEAR_CHUNKS, CHUNKS)
                def _(c):
                    y_copy(side, c).wait_send()

    @pl.when(g > 0)
    def _():
        @pl.loop(0, NEAR_CHUNKS)
        def _(c):
            x_copy(c).wait_send()

    @pl.when(g > 1)
    def _():
        @pl.loop(0, FAR_CHUNKS)
        def _(c):
            far_copy(c).wait_send()


def solution(mesh):
    G, W = mesh.shape["grow"], mesh.shape["wide"]

    def body(fields, melt_planes, slide_planes):
        dma = pltpu.SemaphoreType.DMA
        return pl.pallas_call(
            functools.partial(kernel, G, W),
            out_shape=jax.ShapeDtypeStruct(fields.shape, jnp.float32),
            in_specs=[
                pl.BlockSpec(memory_space=pltpu.SMEM),
                pl.BlockSpec(memory_space=pl.ANY),
                pl.BlockSpec(memory_space=pl.ANY),
            ],
            out_specs=pl.BlockSpec(memory_space=pltpu.VMEM),
            scratch_shapes=[
                pltpu.VMEM((STEPS + 1, 3, PLANES, ROWS, 128), jnp.float32),
                pltpu.VMEM((3, OWN, ROWS, 128), jnp.float32),
                pltpu.SMEM((STEPS + 1,), jnp.int32),
                dma((2,)), dma((CHUNKS,)), dma((CHUNKS,)),
                dma((2, CHUNKS + 1)), dma((2, CHUNKS + 1)), dma((2,)), dma((2,)),
            ],
            compiler_params=pltpu.CompilerParams(
                collective_id=0, has_side_effects=True, vmem_limit_bytes=60 * 1024 * 1024),
        )(slide_planes, fields, melt_planes)

    return jax.shard_map(
        body, mesh=mesh,
        in_specs=(P(None, "grow", "wide", None), P(None, None, "wide", None), P()),
        out_specs=P(None, "grow", "wide", None), check_vma=False)
```

```python
import functools

import jax
import jax.numpy as jnp
from jax import lax
from jax.experimental import pallas as pl
from jax.experimental.pallas import tpu as pltpu
from jax.sharding import PartitionSpec as P

MESH = pl.DeviceIdType.MESH
STEPS = 8
OWN = 16
FAR = 8
PLANES = OWN + OWN + FAR
COLS = 32
LO = 16
ROWS = 64
PAD = 2
CHUNK = 2
NEAR_CHUNKS = OWN // CHUNK
FAR_CHUNK = 4
FAR_CHUNKS = FAR // FAR_CHUNK
CHUNKS = NEAR_CHUNKS + FAR_CHUNKS
GROUP = 4
RING = 4


def kernel(G, W, slide, fields, melt, out, lev, mbuf, rbuf, cur, local_sem,
           x_send, x_recv, r_send, r_recv, y_send, y_recv, m_send, m_recv):
    g = lax.axis_index("grow")
    w = lax.axis_index("wide")
    base = OWN * (G - g)
    has_left, has_right = w > 0, w < W - 1
    start, place = g - g % RING, g % RING
    relay_to = start + (place + 1) % RING
    relay_from = start + (place + RING - 1) % RING
    source = g + 2
    far_from = source - source % RING + (source + 1) % RING
    relays = relay_from > 1
    partners = (
        (g > 0, {"grow": g - 1}), (g < G - 1, {"grow": g + 1}),
        (g > 1, {"grow": relay_to}), (relays, {"grow": relay_from}),
        (relays, {"grow": relay_from - 2}), (g < G - 2, {"grow": far_from}),
        (has_left, {"wide": w - 1}), (has_right, {"wide": w + 1}),
    )
    barrier = pltpu.get_barrier_semaphore()
    count = jnp.int32(0)
    for there, device in partners:
        count = count + there.astype(jnp.int32)

        @pl.when(there)
        def _():
            pl.semaphore_signal(barrier, inc=1, device_id=device, device_id_type=MESH)

    own = pltpu.make_async_copy(fields, lev.at[0, :, pl.ds(PAD + 0, OWN), pl.ds(LO, COLS), :], local_sem.at[0])
    own.start()
    melt_in = pltpu.make_async_copy(melt, mbuf.at[:, :, pl.ds(LO, COLS), :], local_sem.at[1])

    @pl.when(g >= G - 2)
    def _():
        melt_in.start()

    cursor = jnp.int32(0)
    cur[0] = cursor
    for k in range(STEPS):
        cursor = cursor + slide[k]
        cur[k + 1] = cursor

    zeros = jnp.zeros((8, 128), jnp.float32)
    for side_there, row in ((has_left, LO - 8), (has_right, LO + COLS)):

        @pl.when(jnp.logical_not(side_there))
        def _():
            @pl.loop(0, PLANES)
            def _(x):
                for f in range(3):
                    lev[0, f, PAD + x, pl.ds(row, 8), :] = zeros

            @pl.loop(0, OWN)
            def _(x):
                for f in range(3):
                    mbuf[f, x, pl.ds(row, 8), :] = zeros

    def zero_planes(first, last):
        @pl.loop(first, last)
        def _(x):
            for f in range(3):
                for k in range(6):
                    lev[0, f, PAD + x, pl.ds(LO - 8 + 8 * k, 8), :] = zeros

    @pl.when(g == G - 1)
    def _():
        zero_planes(OWN, PLANES)

    @pl.when(g == G - 2)
    def _():
        zero_planes(2 * OWN, PLANES)

    def x_copy(c):
        return pltpu.make_async_remote_copy(
            src_ref=fields.at[:, pl.ds(CHUNK * c, CHUNK)],
            dst_ref=lev.at[0, :, pl.ds(PAD + OWN + CHUNK * c, CHUNK), pl.ds(LO, COLS), :],
            send_sem=x_send.at[c], recv_sem=x_recv.at[c], device_id={"grow": g - 1}, device_id_type=MESH)

    def relay_copy(c):
        return pltpu.make_async_remote_copy(
            src_ref=fields.at[:, pl.ds(FAR_CHUNK * c, FAR_CHUNK)],
            dst_ref=rbuf.at[:, pl.ds(FAR_CHUNK * c, FAR_CHUNK)],
            send_sem=r_send.at[c], recv_sem=r_recv.at[c], device_id={"grow": relay_to}, device_id_type=MESH)

    def far_copy(c):
        return pltpu.make_async_remote_copy(
            src_ref=rbuf.at[:, pl.ds(FAR_CHUNK * c, FAR_CHUNK)],
            dst_ref=lev.at[0, :, pl.ds(PAD + 2 * OWN + FAR_CHUNK * c, FAR_CHUNK), pl.ds(LO, COLS), :],
            send_sem=x_send.at[NEAR_CHUNKS + c], recv_sem=x_recv.at[NEAR_CHUNKS + c],
            device_id={"grow": relay_from - 2}, device_id_type=MESH)

    def y_own(side):
        rows, to, there = ((0, LO + COLS, w - 1), (COLS - 8, LO - 8, w + 1))[side]
        return pltpu.make_async_remote_copy(
            src_ref=fields.at[:, :, pl.ds(rows, 8), :],
            dst_ref=lev.at[0, :, pl.ds(PAD + 0, OWN), pl.ds(to, 8), :],
            send_sem=y_send.at[side, CHUNKS], recv_sem=y_recv.at[side, CHUNKS],
            device_id={"wide": there}, device_id_type=MESH)

    def y_melt(side):
        rows, to, there = ((0, LO + COLS, w - 1), (COLS - 8, LO - 8, w + 1))[side]
        return pltpu.make_async_remote_copy(
            src_ref=melt.at[:, :, pl.ds(rows, 8), :],
            dst_ref=mbuf.at[:, :, pl.ds(to, 8), :],
            send_sem=m_send.at[side], recv_sem=m_recv.at[side],
            device_id={"wide": there}, device_id_type=MESH)

    def y_copy(side, c, far=False):
        rows, to, there = ((LO, LO + COLS, w - 1), (LO + COLS - 8, LO - 8, w + 1))[side]
        size = FAR_CHUNK if far else CHUNK
        x = (2 * OWN if far else OWN) + size * c
        slot = NEAR_CHUNKS + c if far else c
        return pltpu.make_async_remote_copy(
            src_ref=lev.at[0, :, pl.ds(PAD + x, size), pl.ds(rows, 8), :],
            dst_ref=lev.at[0, :, pl.ds(PAD + x, size), pl.ds(to, 8), :],
            send_sem=y_send.at[side, slot], recv_sem=y_recv.at[side, slot],
            device_id={"wide": there}, device_id_type=MESH)

    sends = (has_left, has_right)
    receives = (has_right, has_left)

    pl.semaphore_wait(barrier, count)
    for side in (0, 1):
        @pl.when(sends[side])
        def _():
            y_own(side).start()

    @pl.when(g > 0)
    def _():
        @pl.loop(0, NEAR_CHUNKS)
        def _(c):
            x_copy(c).start()

    @pl.when(g > 1)
    def _():
        @pl.loop(0, FAR_CHUNKS)
        def _(c):
            relay_copy(c).start()

    @pl.when(g >= G - 2)
    def _():
        for side in (0, 1):
            @pl.when(sends[side])
            def _():
                y_melt(side).start()

    def advance(t, x):
        for k in range(6):
            row = LO - 8 + 8 * k
            total, centre = [[] for _ in range(GROUP)], [[] for _ in range(GROUP)]
            for f in range(3):
                along = [lev[t, f, PAD + x + d, pl.ds(row, 8), :] for d in range(-1, GROUP + 1)]
                for q in range(GROUP):
                    here = along[q + 1]
                    around = along[q] + along[q + 2]
                    around = around + lev[t, f, PAD + x + q, pl.ds(row - 1, 8), :] + lev[t, f, PAD + x + q, pl.ds(row + 1, 8), :]
                    around = around + (pltpu.roll(here, 1, 1) + pltpu.roll(here, 127, 1))
                    total[q].append(around)
                    centre[q].append(here)
            for q in range(GROUP):
                p, s, h = centre[q]
                p2 = p * p
                rest = 1.0 - p2
                drive = p * (0.4 - 0.3 * p2) + 0.15 * total[q][0] - rest * rest * (0.4 * h + 0.6 * s)
                grown = jnp.tanh(drive)
                change = 0.5 * (grown - p)
                s = (0.4 * s + 0.1 * total[q][1]) + change
                h = (0.04 * h + 0.16 * total[q][2]) + change
                new = [grown, s, h]
                if k == 0:
                    new = [jnp.where(has_left, v, 0.0) for v in new]
                if k == 5:
                    new = [jnp.where(has_right, v, 0.0) for v in new]
                for f in range(3):
                    lev[t + 1, f, PAD + x + q, pl.ds(row, 8), :] = new[f]

    span = pl.ds(LO - 8, COLS + 16)

    def left_edge(t, x):
        @pl.when(jnp.logical_and(g == 0, x < OWN))
        def _():
            for q in range(GROUP):
                keep = x + q >= cur[t + 1]
                for f in range(3):
                    lev[t + 1, f, PAD + x + q, span, :] = jnp.where(keep, lev[t + 1, f, PAD + x + q, span, :], 0.0)

    def right_edge(t, x):
        for q in range(GROUP):
            @pl.when(x + q >= base)
            def _():
                plane = x + q - base
                inside = cur[t] > plane
                enters = cur[t + 1] > plane
                slot = jnp.minimum(plane, OWN - 1)
                for f in range(3):
                    fresh = jnp.where(enters, mbuf[f, slot, span, :], 0.0)
                    lev[t + 1, f, PAD + x + q, span, :] = jnp.where(inside, lev[t + 1, f, PAD + x + q, span, :], fresh)

    own.wait()
    for side in (0, 1):
        @pl.when(receives[side])
        def _():
            y_own(side).wait_recv()

    @pl.when(g >= G - 2)
    def _():
        melt_in.wait()
        for side in (0, 1):
            @pl.when(receives[side])
            def _():
                y_melt(side).wait_recv()

    @pl.loop(0, STEPS - 1)
    def _(t):
        groups = (OWN - 2 - 2 * t + GROUP - 1) // GROUP

        @pl.loop(0, groups)
        def _(i):
            x = OWN - 1 - t - GROUP * (groups - i)
            advance(t, x)
            left_edge(t, x)

    def pass_on(c, far=False):
        for side in (0, 1):
            @pl.when(sends[side])
            def _():
                y_copy(side, c, far).start()

    def edges_in(c, far=False):
        for side in (0, 1):
            @pl.when(receives[side])
            def _():
                y_copy(side, c, far).wait_recv()

    def arrive(c):
        @pl.when(g < G - 1)
        def _():
            x_copy(c).wait_recv()
            pass_on(c)

    groups = OWN // GROUP
    arrive(0)

    @pl.loop(0, groups)
    def _(j):
        arrive(2 * j + 1)

        @pl.when(jnp.logical_and(j < FAR_CHUNKS, relays))
        def _():
            relay_copy(j).wait_recv()
            far_copy(j).start()

        @pl.when(jnp.logical_and(j >= groups - FAR_CHUNKS, g < G - 2))
        def _():
            c = j - (groups - FAR_CHUNKS)
            far_copy(c).wait_recv()
            pass_on(c, True)

        @pl.when(j < groups - 1)
        def _():
            arrive(2 * j + 2)

        @pl.when(g < G - 1)
        def _():
            edges_in(2 * j)
            edges_in(2 * j + 1)

        @pl.loop(0, STEPS)
        def _(t):
            x = OWN + GROUP * j - 1 - t
            advance(t, x)
            left_edge(t, x)
            right_edge(t, x)

    @pl.when(g < G - 2)
    def _():
        for c in range(FAR_CHUNKS):
            edges_in(c, True)

    @pl.loop(0, STEPS)
    def _(t):
        @pl.loop(0, FAR // GROUP)
        def _(i):
            x = 2 * OWN - 1 - t + GROUP * i
            advance(t, x)
            right_edge(t, x)

    shift = cur[STEPS]
    @pl.loop(0, OWN)
    def _(x):
        for f in range(3):
            out[f, x] = lev[STEPS, f, PAD + shift + x, pl.ds(LO, COLS), :]

    for side in (0, 1):
        @pl.when(sends[side])
        def _():
            y_own(side).wait_send()

            @pl.when(g >= G - 2)
            def _():
                y_melt(side).wait_send()

            @pl.when(g < G - 1)
            def _():
                @pl.loop(0, NEAR_CHUNKS)
                def _(c):
                    y_copy(side, c).wait_send()

            @pl.when(g < G - 2)
            def _():
                for c in range(FAR_CHUNKS):
                    y_copy(side, c, True).wait_send()

    @pl.when(g > 0)
    def _():
        @pl.loop(0, NEAR_CHUNKS)
        def _(c):
            x_copy(c).wait_send()

    for c in range(FAR_CHUNKS):
        @pl.when(g > 1)
        def _():
            relay_copy(c).wait_send()

        @pl.when(relays)
        def _():
            far_copy(c).wait_send()


def solution(mesh):
    G, W = mesh.shape["grow"], mesh.shape["wide"]

    def body(fields, melt_planes, slide_planes):
        dma = pltpu.SemaphoreType.DMA
        return pl.pallas_call(
            functools.partial(kernel, G, W),
            out_shape=jax.ShapeDtypeStruct(fields.shape, jnp.float32),
            in_specs=[
                pl.BlockSpec(memory_space=pltpu.SMEM),
                pl.BlockSpec(memory_space=pl.ANY),
                pl.BlockSpec(memory_space=pl.ANY),
            ],
            out_specs=pl.BlockSpec(memory_space=pltpu.VMEM),
            scratch_shapes=[
                pltpu.VMEM((STEPS + 1, 3, PAD + PLANES, ROWS, 128), jnp.float32),
                pltpu.VMEM((3, OWN, ROWS, 128), jnp.float32),
                pltpu.VMEM((3, FAR, COLS, 128), jnp.float32),
                pltpu.SMEM((STEPS + 1,), jnp.int32),
                dma((2,)), dma((CHUNKS,)), dma((CHUNKS,)), dma((FAR_CHUNKS,)), dma((FAR_CHUNKS,)),
                dma((2, CHUNKS + 1)), dma((2, CHUNKS + 1)), dma((2,)), dma((2,)),
            ],
            compiler_params=pltpu.CompilerParams(
                collective_id=0, has_side_effects=True, vmem_limit_bytes=60 * 1024 * 1024),
        )(slide_planes, fields, melt_planes)

    return jax.shard_map(
        body, mesh=mesh,
        in_specs=(P(None, "grow", "wide", None), P(None, None, "wide", None), P()),
        out_specs=P(None, "grow", "wide", None), check_vma=False)
```

```python
import functools

import jax
import jax.numpy as jnp
from jax import lax
from jax.experimental import pallas as pl
from jax.experimental.pallas import tpu as pltpu
from jax.sharding import PartitionSpec as P

MESH = pl.DeviceIdType.MESH
STEPS = 8
OWN = 16
FAR = 8
PLANES = OWN + OWN + FAR
COLS = 32
LO = 16
ROWS = 64
PAD = 2
CHUNK = 2
NEAR_CHUNKS = OWN // CHUNK
FAR_CHUNK = 4
FAR_CHUNKS = FAR // FAR_CHUNK
CHUNKS = NEAR_CHUNKS + FAR_CHUNKS
GROUP = 4
RING = 4


def kernel(G, W, slide, fields, melt, out, lev, mbuf, rbuf, cur, local_sem,
           x_send, x_recv, r_send, r_recv, y_send, y_recv, m_send, m_recv):
    g = lax.axis_index("grow")
    w = lax.axis_index("wide")
    base = OWN * (G - g)
    has_left, has_right = w > 0, w < W - 1
    start, place = g - g % RING, g % RING
    relay_to = start + (place + 1) % RING
    relay_from = start + (place + RING - 1) % RING
    source = g + 2
    far_from = source - source % RING + (source + 1) % RING
    relays = relay_from > 1
    partners = (
        (g > 0, {"grow": g - 1}), (g < G - 1, {"grow": g + 1}),
        (g > 1, {"grow": relay_to}), (relays, {"grow": relay_from}),
        (relays, {"grow": relay_from - 2}), (g < G - 2, {"grow": far_from}),
        (has_left, {"wide": w - 1}), (has_right, {"wide": w + 1}),
    )
    barrier = pltpu.get_barrier_semaphore()
    count = jnp.int32(0)
    for there, device in partners:
        count = count + there.astype(jnp.int32)

        @pl.when(there)
        def _():
            pl.semaphore_signal(barrier, inc=1, device_id=device, device_id_type=MESH)

    own = pltpu.make_async_copy(fields, lev.at[0, :, pl.ds(PAD + 0, OWN), pl.ds(LO, COLS), :], local_sem.at[0])
    own.start()
    melt_in = pltpu.make_async_copy(melt, mbuf.at[:, :, pl.ds(LO, COLS), :], local_sem.at[1])

    @pl.when(g >= G - 2)
    def _():
        melt_in.start()

    cursor = jnp.int32(0)
    cur[0] = cursor
    for k in range(STEPS):
        cursor = cursor + slide[k]
        cur[k + 1] = cursor

    zeros = jnp.zeros((8, 128), jnp.float32)
    for side_there, row in ((has_left, LO - 8), (has_right, LO + COLS)):

        @pl.when(jnp.logical_not(side_there))
        def _():
            @pl.loop(0, PLANES)
            def _(x):
                for f in range(3):
                    lev[0, f, PAD + x, pl.ds(row, 8), :] = zeros

            @pl.loop(0, OWN)
            def _(x):
                for f in range(3):
                    mbuf[f, x, pl.ds(row, 8), :] = zeros

    def zero_planes(first, last):
        @pl.loop(first, last)
        def _(x):
            for f in range(3):
                for k in range(6):
                    lev[0, f, PAD + x, pl.ds(LO - 8 + 8 * k, 8), :] = zeros

    @pl.when(g == G - 1)
    def _():
        zero_planes(OWN, PLANES)

    @pl.when(g == G - 2)
    def _():
        zero_planes(2 * OWN, PLANES)

    def x_copy(c):
        return pltpu.make_async_remote_copy(
            src_ref=fields.at[:, pl.ds(CHUNK * c, CHUNK)],
            dst_ref=lev.at[0, :, pl.ds(PAD + OWN + CHUNK * c, CHUNK), pl.ds(LO, COLS), :],
            send_sem=x_send.at[c], recv_sem=x_recv.at[c], device_id={"grow": g - 1}, device_id_type=MESH)

    def relay_copy(c):
        return pltpu.make_async_remote_copy(
            src_ref=fields.at[:, pl.ds(FAR_CHUNK * c, FAR_CHUNK)],
            dst_ref=rbuf.at[:, pl.ds(FAR_CHUNK * c, FAR_CHUNK)],
            send_sem=r_send.at[c], recv_sem=r_recv.at[c], device_id={"grow": relay_to}, device_id_type=MESH)

    def far_copy(c):
        return pltpu.make_async_remote_copy(
            src_ref=rbuf.at[:, pl.ds(FAR_CHUNK * c, FAR_CHUNK)],
            dst_ref=lev.at[0, :, pl.ds(PAD + 2 * OWN + FAR_CHUNK * c, FAR_CHUNK), pl.ds(LO, COLS), :],
            send_sem=x_send.at[NEAR_CHUNKS + c], recv_sem=x_recv.at[NEAR_CHUNKS + c],
            device_id={"grow": relay_from - 2}, device_id_type=MESH)

    def y_own(side):
        rows, to, there = ((0, LO + COLS, w - 1), (COLS - 8, LO - 8, w + 1))[side]
        return pltpu.make_async_remote_copy(
            src_ref=fields.at[:, :, pl.ds(rows, 8), :],
            dst_ref=lev.at[0, :, pl.ds(PAD + 0, OWN), pl.ds(to, 8), :],
            send_sem=y_send.at[side, CHUNKS], recv_sem=y_recv.at[side, CHUNKS],
            device_id={"wide": there}, device_id_type=MESH)

    def y_melt(side):
        rows, to, there = ((0, LO + COLS, w - 1), (COLS - 8, LO - 8, w + 1))[side]
        return pltpu.make_async_remote_copy(
            src_ref=melt.at[:, :, pl.ds(rows, 8), :],
            dst_ref=mbuf.at[:, :, pl.ds(to, 8), :],
            send_sem=m_send.at[side], recv_sem=m_recv.at[side],
            device_id={"wide": there}, device_id_type=MESH)

    def y_copy(side, c, far=False):
        rows, to, there = ((LO, LO + COLS, w - 1), (LO + COLS - 8, LO - 8, w + 1))[side]
        size = FAR_CHUNK if far else CHUNK
        x = (2 * OWN if far else OWN) + size * c
        slot = NEAR_CHUNKS + c if far else c
        return pltpu.make_async_remote_copy(
            src_ref=lev.at[0, :, pl.ds(PAD + x, size), pl.ds(rows, 8), :],
            dst_ref=lev.at[0, :, pl.ds(PAD + x, size), pl.ds(to, 8), :],
            send_sem=y_send.at[side, slot], recv_sem=y_recv.at[side, slot],
            device_id={"wide": there}, device_id_type=MESH)

    sends = (has_left, has_right)
    receives = (has_right, has_left)

    pl.semaphore_wait(barrier, count)
    for side in (0, 1):
        @pl.when(sends[side])
        def _():
            y_own(side).start()

    @pl.when(g > 0)
    def _():
        @pl.loop(0, NEAR_CHUNKS)
        def _(c):
            x_copy(c).start()

    @pl.when(g > 1)
    def _():
        @pl.loop(0, FAR_CHUNKS)
        def _(c):
            relay_copy(c).start()

    @pl.when(g >= G - 2)
    def _():
        for side in (0, 1):
            @pl.when(sends[side])
            def _():
                y_melt(side).start()

    def advance(t, x):
        for k in range(6):
            row = LO - 8 + 8 * k
            total, centre = [[] for _ in range(GROUP)], [[] for _ in range(GROUP)]
            for f in range(3):
                along = [lev[t, f, PAD + x + d, pl.ds(row, 8), :] for d in range(-1, GROUP + 1)]
                for q in range(GROUP):
                    here = along[q + 1]
                    around = along[q] + along[q + 2]
                    around = around + lev[t, f, PAD + x + q, pl.ds(row - 1, 8), :] + lev[t, f, PAD + x + q, pl.ds(row + 1, 8), :]
                    around = around + (pltpu.roll(here, 1, 1) + pltpu.roll(here, 127, 1))
                    total[q].append(around)
                    centre[q].append(here)
            for q in range(GROUP):
                p, s, h = centre[q]
                p2 = p * p
                rest = 1.0 - p2
                drive = p * (0.4 - 0.3 * p2) + 0.15 * total[q][0] - rest * rest * (0.4 * h + 0.6 * s)
                grown = jnp.tanh(drive)
                change = 0.5 * (grown - p)
                s = (0.4 * s + 0.1 * total[q][1]) + change
                h = (0.04 * h + 0.16 * total[q][2]) + change
                new = [grown, s, h]
                if k == 0:
                    new = [jnp.where(has_left, v, 0.0) for v in new]
                if k == 5:
                    new = [jnp.where(has_right, v, 0.0) for v in new]
                for f in range(3):
                    lev[t + 1, f, PAD + x + q, pl.ds(row, 8), :] = new[f]

    span = pl.ds(LO - 8, COLS + 16)

    def left_edge(t, x):
        @pl.when(jnp.logical_and(g == 0, x < OWN))
        def _():
            for q in range(GROUP):
                keep = x + q >= cur[t + 1]
                for f in range(3):
                    lev[t + 1, f, PAD + x + q, span, :] = jnp.where(keep, lev[t + 1, f, PAD + x + q, span, :], 0.0)

    def right_edge(t, x):
        for q in range(GROUP):
            @pl.when(x + q >= base)
            def _():
                plane = x + q - base
                inside = cur[t] > plane
                enters = cur[t + 1] > plane
                slot = jnp.minimum(plane, OWN - 1)
                for f in range(3):
                    fresh = jnp.where(enters, mbuf[f, slot, span, :], 0.0)
                    lev[t + 1, f, PAD + x + q, span, :] = jnp.where(inside, lev[t + 1, f, PAD + x + q, span, :], fresh)

    own.wait()
    for side in (0, 1):
        @pl.when(receives[side])
        def _():
            y_own(side).wait_recv()

    @pl.when(g >= G - 2)
    def _():
        melt_in.wait()
        for side in (0, 1):
            @pl.when(receives[side])
            def _():
                y_melt(side).wait_recv()

    @pl.loop(0, STEPS - 1)
    def _(t):
        groups = (OWN - 2 - 2 * t + GROUP - 1) // GROUP

        @pl.loop(0, groups)
        def _(i):
            x = OWN - 1 - t - GROUP * (groups - i)
            advance(t, x)
            left_edge(t, x)

    def pass_on(c, far=False):
        for side in (0, 1):
            @pl.when(sends[side])
            def _():
                y_copy(side, c, far).start()

    def edges_in(c, far=False):
        for side in (0, 1):
            @pl.when(receives[side])
            def _():
                y_copy(side, c, far).wait_recv()

    def arrive(c):
        @pl.when(g < G - 1)
        def _():
            x_copy(c).wait_recv()
            pass_on(c)

    groups = OWN // GROUP
    middle = jnp.logical_or(w == W // 2 - 1, w == W // 2)
    ahead = jnp.where(middle, 5, 3)

    @pl.loop(0, groups)
    def _(j):
        first = jnp.where(j == 0, 0, jnp.minimum(2 * j - 2 + ahead, NEAR_CHUNKS))

        @pl.loop(first, jnp.minimum(2 * j + ahead, NEAR_CHUNKS))
        def _(c):
            arrive(c)

        @pl.when(jnp.logical_and(j < FAR_CHUNKS, relays))
        def _():
            relay_copy(j).wait_recv()
            far_copy(j).start()

        @pl.when(jnp.logical_and(j >= groups - FAR_CHUNKS, g < G - 2))
        def _():
            c = j - (groups - FAR_CHUNKS)
            far_copy(c).wait_recv()
            pass_on(c, True)

        @pl.when(g < G - 1)
        def _():
            edges_in(2 * j)
            edges_in(2 * j + 1)

        @pl.loop(0, STEPS)
        def _(t):
            x = OWN + GROUP * j - 1 - t
            advance(t, x)
            left_edge(t, x)
            right_edge(t, x)

    @pl.when(g < G - 2)
    def _():
        for c in range(FAR_CHUNKS):
            edges_in(c, True)

    @pl.loop(0, STEPS)
    def _(t):
        @pl.loop(0, FAR // GROUP)
        def _(i):
            x = 2 * OWN - 1 - t + GROUP * i
            advance(t, x)
            right_edge(t, x)

    shift = cur[STEPS]
    @pl.loop(0, OWN)
    def _(x):
        for f in range(3):
            out[f, x] = lev[STEPS, f, PAD + shift + x, pl.ds(LO, COLS), :]

    for side in (0, 1):
        @pl.when(sends[side])
        def _():
            y_own(side).wait_send()

            @pl.when(g >= G - 2)
            def _():
                y_melt(side).wait_send()

            @pl.when(g < G - 1)
            def _():
                @pl.loop(0, NEAR_CHUNKS)
                def _(c):
                    y_copy(side, c).wait_send()

            @pl.when(g < G - 2)
            def _():
                for c in range(FAR_CHUNKS):
                    y_copy(side, c, True).wait_send()

    @pl.when(g > 0)
    def _():
        @pl.loop(0, NEAR_CHUNKS)
        def _(c):
            x_copy(c).wait_send()

    for c in range(FAR_CHUNKS):
        @pl.when(g > 1)
        def _():
            relay_copy(c).wait_send()

        @pl.when(relays)
        def _():
            far_copy(c).wait_send()


def solution(mesh):
    G, W = mesh.shape["grow"], mesh.shape["wide"]

    def body(fields, melt_planes, slide_planes):
        dma = pltpu.SemaphoreType.DMA
        return pl.pallas_call(
            functools.partial(kernel, G, W),
            out_shape=jax.ShapeDtypeStruct(fields.shape, jnp.float32),
            in_specs=[
                pl.BlockSpec(memory_space=pltpu.SMEM),
                pl.BlockSpec(memory_space=pl.ANY),
                pl.BlockSpec(memory_space=pl.ANY),
            ],
            out_specs=pl.BlockSpec(memory_space=pltpu.VMEM),
            scratch_shapes=[
                pltpu.VMEM((STEPS + 1, 3, PAD + PLANES, ROWS, 128), jnp.float32),
                pltpu.VMEM((3, OWN, ROWS, 128), jnp.float32),
                pltpu.VMEM((3, FAR, COLS, 128), jnp.float32),
                pltpu.SMEM((STEPS + 1,), jnp.int32),
                dma((2,)), dma((CHUNKS,)), dma((CHUNKS,)), dma((FAR_CHUNKS,)), dma((FAR_CHUNKS,)),
                dma((2, CHUNKS + 1)), dma((2, CHUNKS + 1)), dma((2,)), dma((2,)),
            ],
            compiler_params=pltpu.CompilerParams(
                collective_id=0, has_side_effects=True, vmem_limit_bytes=60 * 1024 * 1024),
        )(slide_planes, fields, melt_planes)

    return jax.shard_map(
        body, mesh=mesh,
        in_specs=(P(None, "grow", "wide", None), P(None, None, "wide", None), P()),
        out_specs=P(None, "grow", "wide", None), check_vma=False)
```

```python
import functools

import jax
import jax.numpy as jnp
from jax import lax
from jax.experimental import pallas as pl
from jax.experimental.pallas import tpu as pltpu
from jax.sharding import PartitionSpec as P

MESH = pl.DeviceIdType.MESH
STEPS = 8
OWN = 16
FAR = 8
PLANES = OWN + OWN + FAR
COLS = 32
LO = 16
ROWS = 64
PAD = 2
CHUNK = 2
NEAR_CHUNKS = OWN // CHUNK
FAR_CHUNK = 4
FAR_CHUNKS = FAR // FAR_CHUNK
CHUNKS = NEAR_CHUNKS + FAR_CHUNKS
GROUP = 4
RING = 4
EARLY = 5


def kernel(G, W, slide, fields, melt, out, lev, mbuf, rbuf, ebuf, cur, local_sem,
           x_send, x_recv, r_send, r_recv, y_send, y_recv, m_send, m_recv, e_send, e_recv):
    g = lax.axis_index("grow")
    w = lax.axis_index("wide")
    base = OWN * (G - g)
    has_left, has_right = w > 0, w < W - 1
    start, place = g - g % RING, g % RING
    relay_to = start + (place + 1) % RING
    relay_from = start + (place + RING - 1) % RING
    source = g + 2
    far_from = source - source % RING + (source + 1) % RING
    relays = relay_from > 1
    partners = (
        (g > 0, {"grow": g - 1}), (g < G - 1, {"grow": g + 1}),
        (g > 1, {"grow": relay_to}), (relays, {"grow": relay_from}),
        (relays, {"grow": relay_from - 2}), (g < G - 2, {"grow": far_from}),
        (has_left, {"wide": w - 1}), (has_right, {"wide": w + 1}),
    )
    barrier = pltpu.get_barrier_semaphore()
    count = jnp.int32(0)
    for there, device in partners:
        count = count + there.astype(jnp.int32)

        @pl.when(there)
        def _():
            pl.semaphore_signal(barrier, inc=1, device_id=device, device_id_type=MESH)

    own = pltpu.make_async_copy(fields, lev.at[0, :, pl.ds(PAD + 0, OWN), pl.ds(LO, COLS), :], local_sem.at[0])
    own.start()
    melt_in = pltpu.make_async_copy(melt, mbuf.at[:, :, pl.ds(LO, COLS), :], local_sem.at[1])

    @pl.when(g >= G - 2)
    def _():
        melt_in.start()

    cursor = jnp.int32(0)
    cur[0] = cursor
    for k in range(STEPS):
        cursor = cursor + slide[k]
        cur[k + 1] = cursor

    zeros = jnp.zeros((8, 128), jnp.float32)
    for side_there, row in ((has_left, LO - 8), (has_right, LO + COLS)):

        @pl.when(jnp.logical_not(side_there))
        def _():
            @pl.loop(0, PLANES)
            def _(x):
                for f in range(3):
                    lev[0, f, PAD + x, pl.ds(row, 8), :] = zeros

            @pl.loop(0, OWN)
            def _(x):
                for f in range(3):
                    mbuf[f, x, pl.ds(row, 8), :] = zeros

    def zero_planes(first, last):
        @pl.loop(first, last)
        def _(x):
            for f in range(3):
                for k in range(6):
                    lev[0, f, PAD + x, pl.ds(LO - 8 + 8 * k, 8), :] = zeros

    @pl.when(g == G - 1)
    def _():
        zero_planes(OWN, PLANES)

    @pl.when(g == G - 2)
    def _():
        zero_planes(2 * OWN, PLANES)

    def x_copy(c):
        return pltpu.make_async_remote_copy(
            src_ref=fields.at[:, pl.ds(CHUNK * c, CHUNK)],
            dst_ref=lev.at[0, :, pl.ds(PAD + OWN + CHUNK * c, CHUNK), pl.ds(LO, COLS), :],
            send_sem=x_send.at[c], recv_sem=x_recv.at[c], device_id={"grow": g - 1}, device_id_type=MESH)

    def relay_copy(c):
        return pltpu.make_async_remote_copy(
            src_ref=fields.at[:, pl.ds(FAR_CHUNK * c, FAR_CHUNK)],
            dst_ref=rbuf.at[:, pl.ds(FAR_CHUNK * c, FAR_CHUNK)],
            send_sem=r_send.at[c], recv_sem=r_recv.at[c], device_id={"grow": relay_to}, device_id_type=MESH)

    def far_copy(c):
        return pltpu.make_async_remote_copy(
            src_ref=rbuf.at[:, pl.ds(FAR_CHUNK * c, FAR_CHUNK)],
            dst_ref=lev.at[0, :, pl.ds(PAD + 2 * OWN + FAR_CHUNK * c, FAR_CHUNK), pl.ds(LO, COLS), :],
            send_sem=x_send.at[NEAR_CHUNKS + c], recv_sem=x_recv.at[NEAR_CHUNKS + c],
            device_id={"grow": relay_from - 2}, device_id_type=MESH)

    middle = (w == W // 2 - 1, w == W // 2)
    edge_rows = (LO + COLS, LO - 8)

    def near_edge(side):
        rows = pl.ds(edge_rows[side], 8)
        return pltpu.make_async_remote_copy(
            src_ref=lev.at[0, :, pl.ds(PAD, OWN), rows, :],
            dst_ref=lev.at[0, :, pl.ds(PAD + OWN, OWN), rows, :],
            send_sem=e_send.at[0], recv_sem=e_recv.at[0], device_id={"grow": g - 1}, device_id_type=MESH)

    def relay_edge(side):
        return pltpu.make_async_remote_copy(
            src_ref=lev.at[0, :, pl.ds(PAD, FAR), pl.ds(edge_rows[side], 8), :],
            dst_ref=ebuf,
            send_sem=e_send.at[1], recv_sem=e_recv.at[1], device_id={"grow": relay_to}, device_id_type=MESH)

    def far_edge(side):
        return pltpu.make_async_remote_copy(
            src_ref=ebuf,
            dst_ref=lev.at[0, :, pl.ds(PAD + 2 * OWN, FAR), pl.ds(edge_rows[side], 8), :],
            send_sem=e_send.at[2], recv_sem=e_recv.at[2], device_id={"grow": relay_from - 2}, device_id_type=MESH)

    def y_own(side):
        rows, to, there = ((0, LO + COLS, w - 1), (COLS - 8, LO - 8, w + 1))[side]
        return pltpu.make_async_remote_copy(
            src_ref=fields.at[:, :, pl.ds(rows, 8), :],
            dst_ref=lev.at[0, :, pl.ds(PAD + 0, OWN), pl.ds(to, 8), :],
            send_sem=y_send.at[side, CHUNKS], recv_sem=y_recv.at[side, CHUNKS],
            device_id={"wide": there}, device_id_type=MESH)

    def y_melt(side):
        rows, to, there = ((0, LO + COLS, w - 1), (COLS - 8, LO - 8, w + 1))[side]
        return pltpu.make_async_remote_copy(
            src_ref=melt.at[:, :, pl.ds(rows, 8), :],
            dst_ref=mbuf.at[:, :, pl.ds(to, 8), :],
            send_sem=m_send.at[side], recv_sem=m_recv.at[side],
            device_id={"wide": there}, device_id_type=MESH)

    def y_copy(side, c, far=False):
        rows, to, there = ((LO, LO + COLS, w - 1), (LO + COLS - 8, LO - 8, w + 1))[side]
        size = FAR_CHUNK if far else CHUNK
        x = (2 * OWN if far else OWN) + size * c
        slot = NEAR_CHUNKS + c if far else c
        return pltpu.make_async_remote_copy(
            src_ref=lev.at[0, :, pl.ds(PAD + x, size), pl.ds(rows, 8), :],
            dst_ref=lev.at[0, :, pl.ds(PAD + x, size), pl.ds(to, 8), :],
            send_sem=y_send.at[side, slot], recv_sem=y_recv.at[side, slot],
            device_id={"wide": there}, device_id_type=MESH)

    sends = (has_left, has_right)
    receives = (has_right, has_left)
    passes = (jnp.logical_and(has_left, w != W // 2), jnp.logical_and(has_right, w != W // 2 - 1))
    gets = (jnp.logical_and(has_right, w != W // 2 - 1), jnp.logical_and(has_left, w != W // 2))

    pl.semaphore_wait(barrier, count)
    for side in (0, 1):
        @pl.when(sends[side])
        def _():
            y_own(side).start()

    @pl.when(g > 0)
    def _():
        @pl.loop(0, jnp.where(jnp.logical_or(*middle), EARLY, NEAR_CHUNKS))
        def _(c):
            x_copy(c).start()

    @pl.when(g > 1)
    def _():
        @pl.loop(0, FAR_CHUNKS)
        def _(c):
            relay_copy(c).start()

    @pl.when(g >= G - 2)
    def _():
        for side in (0, 1):
            @pl.when(sends[side])
            def _():
                y_melt(side).start()

    def advance(t, x):
        for k in range(6):
            row = LO - 8 + 8 * k
            total, centre = [[] for _ in range(GROUP)], [[] for _ in range(GROUP)]
            for f in range(3):
                along = [lev[t, f, PAD + x + d, pl.ds(row, 8), :] for d in range(-1, GROUP + 1)]
                for q in range(GROUP):
                    here = along[q + 1]
                    around = along[q] + along[q + 2]
                    around = around + lev[t, f, PAD + x + q, pl.ds(row - 1, 8), :] + lev[t, f, PAD + x + q, pl.ds(row + 1, 8), :]
                    around = around + (pltpu.roll(here, 1, 1) + pltpu.roll(here, 127, 1))
                    total[q].append(around)
                    centre[q].append(here)
            for q in range(GROUP):
                p, s, h = centre[q]
                p2 = p * p
                rest = 1.0 - p2
                drive = p * (0.4 - 0.3 * p2) + 0.15 * total[q][0] - rest * rest * (0.4 * h + 0.6 * s)
                grown = jnp.tanh(drive)
                change = 0.5 * (grown - p)
                s = (0.4 * s + 0.1 * total[q][1]) + change
                h = (0.04 * h + 0.16 * total[q][2]) + change
                new = [grown, s, h]
                if k == 0:
                    new = [jnp.where(has_left, v, 0.0) for v in new]
                if k == 5:
                    new = [jnp.where(has_right, v, 0.0) for v in new]
                for f in range(3):
                    lev[t + 1, f, PAD + x + q, pl.ds(row, 8), :] = new[f]

    span = pl.ds(LO - 8, COLS + 16)

    def left_edge(t, x):
        @pl.when(jnp.logical_and(g == 0, x < OWN))
        def _():
            for q in range(GROUP):
                keep = x + q >= cur[t + 1]
                for f in range(3):
                    lev[t + 1, f, PAD + x + q, span, :] = jnp.where(keep, lev[t + 1, f, PAD + x + q, span, :], 0.0)

    def right_edge(t, x):
        for q in range(GROUP):
            @pl.when(x + q >= base)
            def _():
                plane = x + q - base
                inside = cur[t] > plane
                enters = cur[t + 1] > plane
                slot = jnp.minimum(plane, OWN - 1)
                for f in range(3):
                    fresh = jnp.where(enters, mbuf[f, slot, span, :], 0.0)
                    lev[t + 1, f, PAD + x + q, span, :] = jnp.where(inside, lev[t + 1, f, PAD + x + q, span, :], fresh)

    own.wait()
    for side in (0, 1):
        @pl.when(receives[side])
        def _():
            y_own(side).wait_recv()

    for side in (0, 1):
        @pl.when(jnp.logical_and(middle[side], g > 0))
        def _():
            near_edge(side).start()

            @pl.loop(EARLY, NEAR_CHUNKS)
            def _(c):
                x_copy(c).start()

        @pl.when(jnp.logical_and(middle[side], g > 1))
        def _():
            relay_edge(side).start()

    @pl.when(g >= G - 2)
    def _():
        melt_in.wait()
        for side in (0, 1):
            @pl.when(receives[side])
            def _():
                y_melt(side).wait_recv()

    @pl.loop(0, STEPS - 1)
    def _(t):
        groups = (OWN - 2 - 2 * t + GROUP - 1) // GROUP

        @pl.loop(0, groups)
        def _(i):
            x = OWN - 1 - t - GROUP * (groups - i)
            advance(t, x)
            left_edge(t, x)

    def pass_on(c, far=False):
        for side in (0, 1):
            @pl.when(passes[side])
            def _():
                y_copy(side, c, far).start()

    def edges_in(c, far=False):
        for side in (0, 1):
            @pl.when(gets[side])
            def _():
                y_copy(side, c, far).wait_recv()

    def arrive(c):
        @pl.when(g < G - 1)
        def _():
            x_copy(c).wait_recv()
            pass_on(c)

    groups = OWN // GROUP
    ahead = 3

    @pl.loop(0, groups)
    def _(j):
        first = jnp.where(j == 0, 0, jnp.minimum(2 * j - 2 + ahead, NEAR_CHUNKS))

        @pl.loop(first, jnp.minimum(2 * j + ahead, NEAR_CHUNKS))
        def _(c):
            arrive(c)

        @pl.when(jnp.logical_and(j < FAR_CHUNKS, relays))
        def _():
            relay_copy(j).wait_recv()
            far_copy(j).start()

        @pl.when(jnp.logical_and(j >= groups - FAR_CHUNKS, g < G - 2))
        def _():
            c = j - (groups - FAR_CHUNKS)
            far_copy(c).wait_recv()
            pass_on(c, True)

        for side in (0, 1):
            @pl.when(jnp.logical_and(jnp.logical_and(middle[side], relays), j == 2))
            def _():
                relay_edge(side).wait_recv()
                far_edge(side).start()

            @pl.when(jnp.logical_and(jnp.logical_and(middle[side], g < G - 1), j == 0))
            def _():
                near_edge(side).wait_recv()

        @pl.when(g < G - 1)
        def _():
            edges_in(2 * j)
            edges_in(2 * j + 1)

        @pl.loop(0, STEPS)
        def _(t):
            x = OWN + GROUP * j - 1 - t
            advance(t, x)
            left_edge(t, x)
            right_edge(t, x)

    @pl.when(g < G - 2)
    def _():
        for c in range(FAR_CHUNKS):
            edges_in(c, True)

        for side in (0, 1):
            @pl.when(middle[side])
            def _():
                far_edge(side).wait_recv()

    @pl.loop(0, STEPS)
    def _(t):
        @pl.loop(0, FAR // GROUP)
        def _(i):
            x = 2 * OWN - 1 - t + GROUP * i
            advance(t, x)
            right_edge(t, x)

    shift = cur[STEPS]
    @pl.loop(0, OWN)
    def _(x):
        for f in range(3):
            out[f, x] = lev[STEPS, f, PAD + shift + x, pl.ds(LO, COLS), :]

    for side in (0, 1):
        @pl.when(sends[side])
        def _():
            y_own(side).wait_send()

            @pl.when(g >= G - 2)
            def _():
                y_melt(side).wait_send()

        @pl.when(jnp.logical_and(passes[side], g < G - 1))
        def _():
            @pl.loop(0, NEAR_CHUNKS)
            def _(c):
                y_copy(side, c).wait_send()

        @pl.when(jnp.logical_and(passes[side], g < G - 2))
        def _():
            for c in range(FAR_CHUNKS):
                y_copy(side, c, True).wait_send()

        @pl.when(jnp.logical_and(middle[side], g > 0))
        def _():
            near_edge(side).wait_send()

        @pl.when(jnp.logical_and(middle[side], g > 1))
        def _():
            relay_edge(side).wait_send()

        @pl.when(jnp.logical_and(middle[side], relays))
        def _():
            far_edge(side).wait_send()

    @pl.when(g > 0)
    def _():
        @pl.loop(0, NEAR_CHUNKS)
        def _(c):
            x_copy(c).wait_send()

    for c in range(FAR_CHUNKS):
        @pl.when(g > 1)
        def _():
            relay_copy(c).wait_send()

        @pl.when(relays)
        def _():
            far_copy(c).wait_send()


def solution(mesh):
    G, W = mesh.shape["grow"], mesh.shape["wide"]

    def body(fields, melt_planes, slide_planes):
        dma = pltpu.SemaphoreType.DMA
        return pl.pallas_call(
            functools.partial(kernel, G, W),
            out_shape=jax.ShapeDtypeStruct(fields.shape, jnp.float32),
            in_specs=[
                pl.BlockSpec(memory_space=pltpu.SMEM),
                pl.BlockSpec(memory_space=pl.ANY),
                pl.BlockSpec(memory_space=pl.ANY),
            ],
            out_specs=pl.BlockSpec(memory_space=pltpu.VMEM),
            scratch_shapes=[
                pltpu.VMEM((STEPS + 1, 3, PAD + PLANES, ROWS, 128), jnp.float32),
                pltpu.VMEM((3, OWN, ROWS, 128), jnp.float32),
                pltpu.VMEM((3, FAR, COLS, 128), jnp.float32),
                pltpu.VMEM((3, FAR, 8, 128), jnp.float32),
                pltpu.SMEM((STEPS + 1,), jnp.int32),
                dma((2,)), dma((CHUNKS,)), dma((CHUNKS,)), dma((FAR_CHUNKS,)), dma((FAR_CHUNKS,)),
                dma((2, CHUNKS + 1)), dma((2, CHUNKS + 1)), dma((2,)), dma((2,)), dma((3,)), dma((3,)),
            ],
            compiler_params=pltpu.CompilerParams(
                collective_id=0, has_side_effects=True, vmem_limit_bytes=60 * 1024 * 1024),
        )(slide_planes, fields, melt_planes)

    return jax.shard_map(
        body, mesh=mesh,
        in_specs=(P(None, "grow", "wide", None), P(None, None, "wide", None), P()),
        out_specs=P(None, "grow", "wide", None), check_vma=False)
```

```python
import functools

import jax
import jax.numpy as jnp
from jax import lax
from jax.experimental import pallas as pl
from jax.experimental.pallas import tpu as pltpu
from jax.sharding import PartitionSpec as P

MESH = pl.DeviceIdType.MESH
STEPS = 8
OWN = 16
FAR = 8
PLANES = OWN + OWN + FAR
COLS = 32
LO = 16
ROWS = 64
PAD = 2
CHUNK = 2
NEAR_CHUNKS = OWN // CHUNK
FAR_CHUNK = 4
FAR_CHUNKS = FAR // FAR_CHUNK
CHUNKS = NEAR_CHUNKS + FAR_CHUNKS
RING = 4
EARLY = 6


def kernel(G, W, slide, fields, melt, out, lev, mbuf, rbuf, ebuf, cur, local_sem,
           x_send, x_recv, r_send, r_recv, y_send, y_recv, m_send, m_recv, e_send, e_recv):
    g = lax.axis_index("grow")
    w = lax.axis_index("wide")
    base = OWN * (G - g)
    has_left, has_right = w > 0, w < W - 1
    start, place = g - g % RING, g % RING
    relay_to = start + (place + 1) % RING
    relay_from = start + (place + RING - 1) % RING
    source = g + 2
    far_from = source - source % RING + (source + 1) % RING
    relays = relay_from > 1
    partners = (
        (g > 0, {"grow": g - 1}), (g < G - 1, {"grow": g + 1}),
        (g > 1, {"grow": relay_to}), (relays, {"grow": relay_from}),
        (relays, {"grow": relay_from - 2}), (g < G - 2, {"grow": far_from}),
        (has_left, {"wide": w - 1}), (has_right, {"wide": w + 1}),
    )
    barrier = pltpu.get_barrier_semaphore()
    count = jnp.int32(0)
    for there, device in partners:
        count = count + there.astype(jnp.int32)

        @pl.when(there)
        def _():
            pl.semaphore_signal(barrier, inc=1, device_id=device, device_id_type=MESH)

    own = pltpu.make_async_copy(fields, lev.at[0, :, pl.ds(PAD + 0, OWN), pl.ds(LO, COLS), :], local_sem.at[0])
    own.start()
    melt_in = pltpu.make_async_copy(melt, mbuf.at[:, :, pl.ds(LO, COLS), :], local_sem.at[1])

    @pl.when(g >= G - 2)
    def _():
        melt_in.start()

    cursor = jnp.int32(0)
    cur[0] = cursor
    for k in range(STEPS):
        cursor = cursor + slide[k]
        cur[k + 1] = cursor

    zeros = jnp.zeros((8, 128), jnp.float32)
    for side_there, row in ((has_left, LO - 8), (has_right, LO + COLS)):

        @pl.when(jnp.logical_not(side_there))
        def _():
            @pl.loop(0, PLANES)
            def _(x):
                for f in range(3):
                    lev[0, f, PAD + x, pl.ds(row, 8), :] = zeros

            @pl.loop(0, OWN)
            def _(x):
                for f in range(3):
                    mbuf[f, x, pl.ds(row, 8), :] = zeros

    def zero_planes(first, last):
        @pl.loop(first, last)
        def _(x):
            for f in range(3):
                for k in range(6):
                    lev[0, f, PAD + x, pl.ds(LO - 8 + 8 * k, 8), :] = zeros

    @pl.when(g == G - 1)
    def _():
        zero_planes(OWN, PLANES)

    @pl.when(g == G - 2)
    def _():
        zero_planes(2 * OWN, PLANES)

    def x_copy(c):
        return pltpu.make_async_remote_copy(
            src_ref=fields.at[:, pl.ds(CHUNK * c, CHUNK)],
            dst_ref=lev.at[0, :, pl.ds(PAD + OWN + CHUNK * c, CHUNK), pl.ds(LO, COLS), :],
            send_sem=x_send.at[c], recv_sem=x_recv.at[c], device_id={"grow": g - 1}, device_id_type=MESH)

    def relay_copy(c):
        return pltpu.make_async_remote_copy(
            src_ref=fields.at[:, pl.ds(FAR_CHUNK * c, FAR_CHUNK)],
            dst_ref=rbuf.at[:, pl.ds(FAR_CHUNK * c, FAR_CHUNK)],
            send_sem=r_send.at[c], recv_sem=r_recv.at[c], device_id={"grow": relay_to}, device_id_type=MESH)

    def far_copy(c):
        return pltpu.make_async_remote_copy(
            src_ref=rbuf.at[:, pl.ds(FAR_CHUNK * c, FAR_CHUNK)],
            dst_ref=lev.at[0, :, pl.ds(PAD + 2 * OWN + FAR_CHUNK * c, FAR_CHUNK), pl.ds(LO, COLS), :],
            send_sem=x_send.at[NEAR_CHUNKS + c], recv_sem=x_recv.at[NEAR_CHUNKS + c],
            device_id={"grow": relay_from - 2}, device_id_type=MESH)

    middle = (w == W // 2 - 1, w == W // 2)
    edge_rows = (LO + COLS, LO - 8)

    def near_edge(side):
        rows = pl.ds(edge_rows[side], 8)
        return pltpu.make_async_remote_copy(
            src_ref=lev.at[0, :, pl.ds(PAD, OWN), rows, :],
            dst_ref=lev.at[0, :, pl.ds(PAD + OWN, OWN), rows, :],
            send_sem=e_send.at[0], recv_sem=e_recv.at[0], device_id={"grow": g - 1}, device_id_type=MESH)

    def relay_edge(side):
        return pltpu.make_async_remote_copy(
            src_ref=lev.at[0, :, pl.ds(PAD, FAR), pl.ds(edge_rows[side], 8), :],
            dst_ref=ebuf,
            send_sem=e_send.at[1], recv_sem=e_recv.at[1], device_id={"grow": relay_to}, device_id_type=MESH)

    def far_edge(side):
        return pltpu.make_async_remote_copy(
            src_ref=ebuf,
            dst_ref=lev.at[0, :, pl.ds(PAD + 2 * OWN, FAR), pl.ds(edge_rows[side], 8), :],
            send_sem=e_send.at[2], recv_sem=e_recv.at[2], device_id={"grow": relay_from - 2}, device_id_type=MESH)

    def y_own(side):
        rows, to, there = ((0, LO + COLS, w - 1), (COLS - 8, LO - 8, w + 1))[side]
        return pltpu.make_async_remote_copy(
            src_ref=fields.at[:, :, pl.ds(rows, 8), :],
            dst_ref=lev.at[0, :, pl.ds(PAD + 0, OWN), pl.ds(to, 8), :],
            send_sem=y_send.at[side, CHUNKS], recv_sem=y_recv.at[side, CHUNKS],
            device_id={"wide": there}, device_id_type=MESH)

    def y_melt(side):
        rows, to, there = ((0, LO + COLS, w - 1), (COLS - 8, LO - 8, w + 1))[side]
        return pltpu.make_async_remote_copy(
            src_ref=melt.at[:, :, pl.ds(rows, 8), :],
            dst_ref=mbuf.at[:, :, pl.ds(to, 8), :],
            send_sem=m_send.at[side], recv_sem=m_recv.at[side],
            device_id={"wide": there}, device_id_type=MESH)

    def y_copy(side, c, far=False):
        rows, to, there = ((LO, LO + COLS, w - 1), (LO + COLS - 8, LO - 8, w + 1))[side]
        size = FAR_CHUNK if far else CHUNK
        x = (2 * OWN if far else OWN) + size * c
        slot = NEAR_CHUNKS + c if far else c
        return pltpu.make_async_remote_copy(
            src_ref=lev.at[0, :, pl.ds(PAD + x, size), pl.ds(rows, 8), :],
            dst_ref=lev.at[0, :, pl.ds(PAD + x, size), pl.ds(to, 8), :],
            send_sem=y_send.at[side, slot], recv_sem=y_recv.at[side, slot],
            device_id={"wide": there}, device_id_type=MESH)

    sends = (has_left, has_right)
    receives = (has_right, has_left)
    passes = (jnp.logical_and(has_left, w != W // 2), jnp.logical_and(has_right, w != W // 2 - 1))
    gets = (jnp.logical_and(has_right, w != W // 2 - 1), jnp.logical_and(has_left, w != W // 2))

    pl.semaphore_wait(barrier, count)
    for side in (0, 1):
        @pl.when(sends[side])
        def _():
            y_own(side).start()

    @pl.when(g > 0)
    def _():
        @pl.loop(0, jnp.where(jnp.logical_or(*middle), EARLY, NEAR_CHUNKS))
        def _(c):
            x_copy(c).start()

    @pl.when(g > 1)
    def _():
        @pl.loop(0, FAR_CHUNKS)
        def _(c):
            relay_copy(c).start()

    @pl.when(g >= G - 2)
    def _():
        for side in (0, 1):
            @pl.when(sends[side])
            def _():
                y_melt(side).start()

    def advance(t, x, n):
        for k in range(6):
            row = LO - 8 + 8 * k
            total, centre = [[] for _ in range(n)], [[] for _ in range(n)]
            for f in range(3):
                along = [lev[t, f, PAD + x + d, pl.ds(row, 8), :] for d in range(-1, n + 1)]
                for q in range(n):
                    here = along[q + 1]
                    around = along[q] + along[q + 2]
                    around = around + lev[t, f, PAD + x + q, pl.ds(row - 1, 8), :] + lev[t, f, PAD + x + q, pl.ds(row + 1, 8), :]
                    around = around + (pltpu.roll(here, 1, 1) + pltpu.roll(here, 127, 1))
                    total[q].append(around)
                    centre[q].append(here)
            for q in range(n):
                p, s, h = centre[q]
                p2 = p * p
                rest = 1.0 - p2
                drive = p * (0.4 - 0.3 * p2) + 0.15 * total[q][0] - rest * rest * (0.4 * h + 0.6 * s)
                grown = jnp.tanh(drive)
                change = 0.5 * (grown - p)
                s = (0.4 * s + 0.1 * total[q][1]) + change
                h = (0.04 * h + 0.16 * total[q][2]) + change
                new = [grown, s, h]
                if k == 0:
                    new = [jnp.where(has_left, v, 0.0) for v in new]
                if k == 5:
                    new = [jnp.where(has_right, v, 0.0) for v in new]
                for f in range(3):
                    lev[t + 1, f, PAD + x + q, pl.ds(row, 8), :] = new[f]

    span = pl.ds(LO - 8, COLS + 16)

    def left_edge(t, x, n):
        @pl.when(jnp.logical_and(g == 0, x < OWN))
        def _():
            for q in range(n):
                keep = x + q >= cur[t + 1]
                for f in range(3):
                    lev[t + 1, f, PAD + x + q, span, :] = jnp.where(keep, lev[t + 1, f, PAD + x + q, span, :], 0.0)

    def right_edge(t, x, n):
        @pl.when(x + n > base)
        def _():
            before, after = cur[t], cur[t + 1]
            for q in range(n):
                plane = x + q - base
                slot = jnp.clip(plane, 0, OWN - 1)
                inside = before > plane
                enters = after > plane
                for f in range(3):
                    fresh = jnp.where(enters, mbuf[f, slot, span, :], 0.0)
                    lev[t + 1, f, PAD + x + q, span, :] = jnp.where(inside, lev[t + 1, f, PAD + x + q, span, :], fresh)

    def pass_on(c, far=False):
        for side in (0, 1):
            @pl.when(passes[side])
            def _():
                y_copy(side, c, far).start()

    def edges_in(c, far=False):
        for side in (0, 1):
            @pl.when(gets[side])
            def _():
                y_copy(side, c, far).wait_recv()

    def arrive(first, last):
        @pl.when(g < G - 1)
        def _():
            @pl.loop(first, last)
            def _(c):
                x_copy(c).wait_recv()
                pass_on(c)

    def arrive_far(c):
        @pl.when(g < G - 2)
        def _():
            far_copy(c).wait_recv()
            pass_on(c, True)

    def hand_over(c):
        @pl.when(relays)
        def _():
            relay_copy(c).wait_recv()
            far_copy(c).start()

    def edges(first, last):
        @pl.when(g < G - 1)
        def _():
            @pl.loop(first, last)
            def _(c):
                edges_in(c)

    def wave(first, n):
        @pl.loop(0, STEPS)
        def _(t):
            x = first - 1 - t
            advance(t, x, n)
            if first <= OWN + STEPS:
                left_edge(t, x, n)
            right_edge(t, x, n)

    def start_of_stream():
        arrive(0, 2)
        hand_over(0)
        arrive(2, 4)

    in_middle = jnp.logical_or(*middle)
    own.wait()

    @pl.when(in_middle)
    def _():
        start_of_stream()

    for side in (0, 1):
        @pl.when(receives[side])
        def _():
            y_own(side).wait_recv()

    for side in (0, 1):
        @pl.when(jnp.logical_and(middle[side], g > 0))
        def _():
            near_edge(side).start()

            @pl.loop(EARLY, NEAR_CHUNKS)
            def _(c):
                x_copy(c).start()

        @pl.when(jnp.logical_and(middle[side], g > 1))
        def _():
            relay_edge(side).start()

    @pl.when(g >= G - 2)
    def _():
        melt_in.wait()
        for side in (0, 1):
            @pl.when(receives[side])
            def _():
                y_melt(side).wait_recv()

    @pl.loop(0, STEPS - 1)
    def _(t):
        groups = (OWN - 2 - 2 * t + 3) // 4

        @pl.loop(0, groups)
        def _(i):
            x = OWN - 1 - t - 4 * (groups - i)
            advance(t, x, 4)
            left_edge(t, x, 4)

    @pl.when(jnp.logical_not(in_middle))
    def _():
        start_of_stream()

    hand_over(1)
    arrive(4, 5)
    for side in (0, 1):
        @pl.when(jnp.logical_and(middle[side], relays))
        def _():
            relay_edge(side).wait_recv()
            far_edge(side).start()

        @pl.when(jnp.logical_and(middle[side], g < G - 1))
        def _():
            near_edge(side).wait_recv()

    edges(0, 4)
    wave(OWN, 8)
    arrive(5, 7)
    arrive_far(0)
    edges(4, 6)
    wave(OWN + 8, 4)
    arrive(7, 8)
    arrive_far(1)
    edges(6, 8)
    wave(OWN + 12, 4)

    @pl.when(g < G - 2)
    def _():
        for c in range(FAR_CHUNKS):
            edges_in(c, True)

        for side in (0, 1):
            @pl.when(middle[side])
            def _():
                far_edge(side).wait_recv()

    wave(2 * OWN, 8)

    shift = cur[STEPS]
    @pl.loop(0, OWN)
    def _(x):
        for f in range(3):
            out[f, x] = lev[STEPS, f, PAD + shift + x, pl.ds(LO, COLS), :]

    for side in (0, 1):
        @pl.when(sends[side])
        def _():
            y_own(side).wait_send()

            @pl.when(g >= G - 2)
            def _():
                y_melt(side).wait_send()

        @pl.when(jnp.logical_and(passes[side], g < G - 1))
        def _():
            @pl.loop(0, NEAR_CHUNKS)
            def _(c):
                y_copy(side, c).wait_send()

        @pl.when(jnp.logical_and(passes[side], g < G - 2))
        def _():
            for c in range(FAR_CHUNKS):
                y_copy(side, c, True).wait_send()

        @pl.when(jnp.logical_and(middle[side], g > 0))
        def _():
            near_edge(side).wait_send()

        @pl.when(jnp.logical_and(middle[side], g > 1))
        def _():
            relay_edge(side).wait_send()

        @pl.when(jnp.logical_and(middle[side], relays))
        def _():
            far_edge(side).wait_send()

    @pl.when(g > 0)
    def _():
        @pl.loop(0, NEAR_CHUNKS)
        def _(c):
            x_copy(c).wait_send()

    for c in range(FAR_CHUNKS):
        @pl.when(g > 1)
        def _():
            relay_copy(c).wait_send()

        @pl.when(relays)
        def _():
            far_copy(c).wait_send()


def solution(mesh):
    G, W = mesh.shape["grow"], mesh.shape["wide"]

    def body(fields, melt_planes, slide_planes):
        dma = pltpu.SemaphoreType.DMA
        return pl.pallas_call(
            functools.partial(kernel, G, W),
            out_shape=jax.ShapeDtypeStruct(fields.shape, jnp.float32),
            in_specs=[
                pl.BlockSpec(memory_space=pltpu.SMEM),
                pl.BlockSpec(memory_space=pl.ANY),
                pl.BlockSpec(memory_space=pl.ANY),
            ],
            out_specs=pl.BlockSpec(memory_space=pltpu.VMEM),
            scratch_shapes=[
                pltpu.VMEM((STEPS + 1, 3, PAD + PLANES, ROWS, 128), jnp.float32),
                pltpu.VMEM((3, OWN, ROWS, 128), jnp.float32),
                pltpu.VMEM((3, FAR, COLS, 128), jnp.float32),
                pltpu.VMEM((3, FAR, 8, 128), jnp.float32),
                pltpu.SMEM((STEPS + 1,), jnp.int32),
                dma((2,)), dma((CHUNKS,)), dma((CHUNKS,)), dma((FAR_CHUNKS,)), dma((FAR_CHUNKS,)),
                dma((2, CHUNKS + 1)), dma((2, CHUNKS + 1)), dma((2,)), dma((2,)), dma((3,)), dma((3,)),
            ],
            compiler_params=pltpu.CompilerParams(
                collective_id=0, has_side_effects=True, vmem_limit_bytes=60 * 1024 * 1024),
        )(slide_planes, fields, melt_planes)

    return jax.shard_map(
        body, mesh=mesh,
        in_specs=(P(None, "grow", "wide", None), P(None, None, "wide", None), P()),
        out_specs=P(None, "grow", "wide", None), check_vma=False)
```

```python
import functools

import jax
import jax.numpy as jnp
from jax import lax
from jax.experimental import pallas as pl
from jax.experimental.pallas import tpu as pltpu
from jax.sharding import PartitionSpec as P

MESH = pl.DeviceIdType.MESH
STEPS = 8
OWN = 16
FAR = 8
PLANES = OWN + OWN + FAR
COLS = 32
LO = 16
ROWS = 64
PAD = 2
HALF = 8
QUAD = 4
RING = 4


def kernel(G, W, slide, fields, melt, out, lev, mbuf, rbuf, ebuf, cur, local_sem,
           n_send, n_recv, r_send, r_recv, f_send, f_recv, y_send, y_recv, m_send, m_recv, e_send, e_recv):
    g = lax.axis_index("grow")
    w = lax.axis_index("wide")
    base = OWN * (G - g)
    has_left, has_right = w > 0, w < W - 1
    start, place = g - g % RING, g % RING
    relay_to = start + (place + 1) % RING
    relay_from = start + (place + RING - 1) % RING
    source = g + 2
    far_from = source - source % RING + (source + 1) % RING
    relays = relay_from > 1
    partners = (
        (g > 0, {"grow": g - 1}), (g < G - 1, {"grow": g + 1}),
        (g > 1, {"grow": relay_to}), (relays, {"grow": relay_from}),
        (relays, {"grow": relay_from - 2}), (g < G - 2, {"grow": far_from}),
        (has_left, {"wide": w - 1}), (has_right, {"wide": w + 1}),
    )
    barrier = pltpu.get_barrier_semaphore()
    count = jnp.int32(0)
    for there, device in partners:
        count = count + there.astype(jnp.int32)

        @pl.when(there)
        def _():
            pl.semaphore_signal(barrier, inc=1, device_id=device, device_id_type=MESH)

    own = pltpu.make_async_copy(fields, lev.at[0, :, pl.ds(PAD + 0, OWN), pl.ds(LO, COLS), :], local_sem.at[0])
    own.start()
    melt_in = pltpu.make_async_copy(melt, mbuf.at[:, :, pl.ds(LO, COLS), :], local_sem.at[1])

    @pl.when(g >= G - 2)
    def _():
        melt_in.start()

    cursor = jnp.int32(0)
    cur[0] = cursor
    for k in range(STEPS):
        cursor = cursor + slide[k]
        cur[k + 1] = cursor

    zeros = jnp.zeros((8, 128), jnp.float32)
    for side_there, row in ((has_left, LO - 8), (has_right, LO + COLS)):

        @pl.when(jnp.logical_not(side_there))
        def _():
            @pl.loop(0, PLANES)
            def _(x):
                for f in range(3):
                    lev[0, f, PAD + x, pl.ds(row, 8), :] = zeros

            @pl.loop(0, OWN)
            def _(x):
                for f in range(3):
                    mbuf[f, x, pl.ds(row, 8), :] = zeros

    def zero_planes(first, last):
        @pl.loop(first, last)
        def _(x):
            for f in range(3):
                for k in range(6):
                    lev[0, f, PAD + x, pl.ds(LO - 8 + 8 * k, 8), :] = zeros

    @pl.when(g == G - 1)
    def _():
        zero_planes(OWN, PLANES)

    @pl.when(g == G - 2)
    def _():
        zero_planes(2 * OWN, PLANES)

    def remote(src, dst, sems, index, device):
        return pltpu.make_async_remote_copy(
            src_ref=src, dst_ref=dst, send_sem=sems[0].at[index], recv_sem=sems[1].at[index],
            device_id=device, device_id_type=MESH)

    def near(part):
        if part < 4:
            first, planes, row, rows = HALF * (part // 2), HALF, (COLS - 8) * (part % 2), 8
        else:
            first, planes, row, rows = QUAD * (part - 4), QUAD, 8, COLS - 16
        return remote(fields.at[:, pl.ds(first, planes), pl.ds(row, rows), :],
                      lev.at[0, :, pl.ds(PAD + OWN + first, planes), pl.ds(LO + row, rows), :],
                      (n_send, n_recv), part, {"grow": g - 1})

    far_rows = ((0, 8), (COLS - 8, 8), (8, COLS - 16))

    def relay(part):
        rows = pl.ds(*far_rows[part])
        return remote(fields.at[:, pl.ds(0, FAR), rows, :], rbuf.at[:, :, rows, :],
                      (r_send, r_recv), part, {"grow": relay_to})

    def far(part):
        row, rows = far_rows[part]
        return remote(rbuf.at[:, :, pl.ds(row, rows), :],
                      lev.at[0, :, pl.ds(PAD + 2 * OWN, FAR), pl.ds(LO + row, rows), :],
                      (f_send, f_recv), part, {"grow": relay_from - 2})

    middle = (w == W // 2 - 1, w == W // 2)
    in_middle = jnp.logical_or(*middle)

    def halo(first, planes, side):
        return lev.at[0, :, pl.ds(PAD + first, planes), pl.ds((LO + COLS, LO - 8)[side], 8), :]

    def near_halo(side):
        return remote(halo(0, OWN, side), halo(OWN, OWN, side), (e_send, e_recv), 0, {"grow": g - 1})

    def relay_halo(side):
        return remote(halo(0, FAR, side), ebuf, (e_send, e_recv), 1, {"grow": relay_to})

    def far_halo(side):
        return remote(ebuf, halo(2 * OWN, FAR, side), (e_send, e_recv), 2, {"grow": relay_from - 2})

    def y_own(side):
        rows, to, there = ((0, LO + COLS, w - 1), (COLS - 8, LO - 8, w + 1))[side]
        return pltpu.make_async_remote_copy(
            src_ref=fields.at[:, :, pl.ds(rows, 8), :],
            dst_ref=lev.at[0, :, pl.ds(PAD + 0, OWN), pl.ds(to, 8), :],
            send_sem=y_send.at[side, 3], recv_sem=y_recv.at[side, 3],
            device_id={"wide": there}, device_id_type=MESH)

    def y_melt(side):
        rows, to, there = ((0, LO + COLS, w - 1), (COLS - 8, LO - 8, w + 1))[side]
        return pltpu.make_async_remote_copy(
            src_ref=melt.at[:, :, pl.ds(rows, 8), :],
            dst_ref=mbuf.at[:, :, pl.ds(to, 8), :],
            send_sem=m_send.at[side], recv_sem=m_recv.at[side],
            device_id={"wide": there}, device_id_type=MESH)

    def y_copy(side, c):
        row, to, there = ((LO, LO + COLS, w - 1), (LO + COLS - 8, LO - 8, w + 1))[side]
        planes = pl.ds(PAD + OWN + HALF * c, HALF)
        return remote(lev.at[0, :, planes, pl.ds(row, 8), :], lev.at[0, :, planes, pl.ds(to, 8), :],
                      (y_send.at[side], y_recv.at[side]), c, {"wide": there})

    sends = (has_left, has_right)
    receives = (has_right, has_left)
    passes = (jnp.logical_and(has_left, w != W // 2), jnp.logical_and(has_right, w != W // 2 - 1))
    gets = (jnp.logical_and(has_right, w != W // 2 - 1), jnp.logical_and(has_left, w != W // 2))

    pl.semaphore_wait(barrier, count)
    for side in (0, 1):
        @pl.when(sends[side])
        def _():
            y_own(side).start()

    @pl.when(g > 0)
    def _():
        for part in range(6):
            near(part).start()

        @pl.when(jnp.logical_not(in_middle))
        def _():
            for part in range(6, 8):
                near(part).start()

    @pl.when(g > 1)
    def _():
        for part in range(3):
            relay(part).start()

    @pl.when(g >= G - 2)
    def _():
        for side in (0, 1):
            @pl.when(sends[side])
            def _():
                y_melt(side).start()

    def advance(t, x, n):
        for k in range(6):
            row = LO - 8 + 8 * k
            total, centre = [[] for _ in range(n)], [[] for _ in range(n)]
            for f in range(3):
                along = [lev[t, f, PAD + x + d, pl.ds(row, 8), :] for d in range(-1, n + 1)]
                for q in range(n):
                    here = along[q + 1]
                    around = along[q] + along[q + 2]
                    around = around + lev[t, f, PAD + x + q, pl.ds(row - 1, 8), :] + lev[t, f, PAD + x + q, pl.ds(row + 1, 8), :]
                    around = around + (pltpu.roll(here, 1, 1) + pltpu.roll(here, 127, 1))
                    total[q].append(around)
                    centre[q].append(here)
            for q in range(n):
                p, s, h = centre[q]
                p2 = p * p
                rest = 1.0 - p2
                drive = p * (0.4 - 0.3 * p2) + 0.15 * total[q][0] - rest * rest * (0.4 * h + 0.6 * s)
                grown = jnp.tanh(drive)
                change = 0.5 * (grown - p)
                s = (0.4 * s + 0.1 * total[q][1]) + change
                h = (0.04 * h + 0.16 * total[q][2]) + change
                new = [grown, s, h]
                if k == 0:
                    new = [jnp.where(has_left, v, 0.0) for v in new]
                if k == 5:
                    new = [jnp.where(has_right, v, 0.0) for v in new]
                for f in range(3):
                    lev[t + 1, f, PAD + x + q, pl.ds(row, 8), :] = new[f]

    span = pl.ds(LO - 8, COLS + 16)

    def left_edge(t, x, n):
        @pl.when(jnp.logical_and(g == 0, x < OWN))
        def _():
            for q in range(n):
                keep = x + q >= cur[t + 1]
                for f in range(3):
                    lev[t + 1, f, PAD + x + q, span, :] = jnp.where(keep, lev[t + 1, f, PAD + x + q, span, :], 0.0)

    def right_edge(t, x, n):
        @pl.when(x + n > base)
        def _():
            before, after = cur[t], cur[t + 1]
            for q in range(n):
                plane = x + q - base
                slot = jnp.clip(plane, 0, OWN - 1)
                inside = before > plane
                enters = after > plane
                for f in range(3):
                    fresh = jnp.where(enters, mbuf[f, slot, span, :], 0.0)
                    lev[t + 1, f, PAD + x + q, span, :] = jnp.where(inside, lev[t + 1, f, PAD + x + q, span, :], fresh)

    def pass_on(c, copies):
        for side in (0, 1):
            copies[side].wait_recv()

            @pl.when(passes[side])
            def _():
                y_copy(side, c).start()

    def near_edges(half):
        @pl.when(g < G - 1)
        def _():
            pass_on(half, (near(2 * half), near(2 * half + 1)))

    def far_edges():
        @pl.when(g < G - 2)
        def _():
            pass_on(2, (far(0), far(1)))

    def hand_over(*parts):
        @pl.when(relays)
        def _():
            for part in parts:
                relay(part).wait_recv()
                far(part).start()

    def edges_in(c):
        for side in (0, 1):
            @pl.when(gets[side])
            def _():
                y_copy(side, c).wait_recv()

    near_edges(0)
    hand_over(0, 1)
    near_edges(1)

    own.wait()
    for side in (0, 1):
        @pl.when(receives[side])
        def _():
            y_own(side).wait_recv()

    for side in (0, 1):
        @pl.when(jnp.logical_and(middle[side], g > 0))
        def _():
            near_halo(side).start()
            for part in range(6, 8):
                near(part).start()

        @pl.when(jnp.logical_and(middle[side], g > 1))
        def _():
            relay_halo(side).start()

    @pl.when(in_middle)
    def _():
        hand_over(2)
        far_edges()

    @pl.when(g >= G - 2)
    def _():
        melt_in.wait()
        for side in (0, 1):
            @pl.when(receives[side])
            def _():
                y_melt(side).wait_recv()

    @pl.loop(0, STEPS - 1)
    def _(t):
        groups = (OWN - 2 - 2 * t + 3) // 4

        @pl.loop(0, groups)
        def _(i):
            x = OWN - 1 - t - 4 * (groups - i)
            advance(t, x, 4)
            left_edge(t, x, 4)

    @pl.when(jnp.logical_not(in_middle))
    def _():
        hand_over(2)

    for side in (0, 1):
        @pl.when(jnp.logical_and(middle[side], relays))
        def _():
            relay_halo(side).wait_recv()
            far_halo(side).start()

    @pl.loop(0, 5)
    def _(stage):
        for k in range(4):
            @pl.when(jnp.logical_and(stage == k, g < G - 1))
            def _():
                near(4 + k).wait_recv()
                if k % 2 == 0:
                    edges_in(k // 2)

        @pl.when(jnp.logical_and(stage == 0, jnp.logical_not(in_middle)))
        def _():
            far_edges()

        for side in (0, 1):
            @pl.when(jnp.logical_and(jnp.logical_and(stage == 0, g < G - 1), middle[side]))
            def _():
                near_halo(side).wait_recv()

        @pl.when(jnp.logical_and(stage == 4, g < G - 2))
        def _():
            far(2).wait_recv()
            edges_in(2)
            for side in (0, 1):
                @pl.when(middle[side])
                def _():
                    far_halo(side).wait_recv()

        first = OWN + QUAD * stage
        parts = jnp.where(stage == 4, 2, 1)

        @pl.loop(0, STEPS)
        def _(t):
            @pl.loop(0, parts)
            def _(i):
                x = first - 1 - t + QUAD * i
                advance(t, x, QUAD)
                left_edge(t, x, QUAD)
                right_edge(t, x, QUAD)

    shift = cur[STEPS]
    @pl.loop(0, OWN)
    def _(x):
        for f in range(3):
            out[f, x] = lev[STEPS, f, PAD + shift + x, pl.ds(LO, COLS), :]

    for side in (0, 1):
        @pl.when(sends[side])
        def _():
            y_own(side).wait_send()

            @pl.when(g >= G - 2)
            def _():
                y_melt(side).wait_send()

        @pl.when(jnp.logical_and(passes[side], g < G - 1))
        def _():
            y_copy(side, 0).wait_send()
            y_copy(side, 1).wait_send()

        @pl.when(jnp.logical_and(passes[side], g < G - 2))
        def _():
            y_copy(side, 2).wait_send()

        @pl.when(jnp.logical_and(middle[side], g > 0))
        def _():
            near_halo(side).wait_send()

        @pl.when(jnp.logical_and(middle[side], g > 1))
        def _():
            relay_halo(side).wait_send()

        @pl.when(jnp.logical_and(middle[side], relays))
        def _():
            far_halo(side).wait_send()

    @pl.when(g > 0)
    def _():
        for part in range(8):
            near(part).wait_send()

    for part in range(3):
        @pl.when(g > 1)
        def _():
            relay(part).wait_send()

        @pl.when(relays)
        def _():
            far(part).wait_send()


def solution(mesh):
    G, W = mesh.shape["grow"], mesh.shape["wide"]

    def body(fields, melt_planes, slide_planes):
        dma = pltpu.SemaphoreType.DMA
        return pl.pallas_call(
            functools.partial(kernel, G, W),
            out_shape=jax.ShapeDtypeStruct(fields.shape, jnp.float32),
            in_specs=[
                pl.BlockSpec(memory_space=pltpu.SMEM),
                pl.BlockSpec(memory_space=pl.ANY),
                pl.BlockSpec(memory_space=pl.ANY),
            ],
            out_specs=pl.BlockSpec(memory_space=pltpu.VMEM),
            scratch_shapes=[
                pltpu.VMEM((STEPS + 1, 3, PAD + PLANES, ROWS, 128), jnp.float32),
                pltpu.VMEM((3, OWN, ROWS, 128), jnp.float32),
                pltpu.VMEM((3, FAR, COLS, 128), jnp.float32),
                pltpu.VMEM((3, FAR, 8, 128), jnp.float32),
                pltpu.SMEM((STEPS + 1,), jnp.int32),
                dma((2,)), dma((8,)), dma((8,)), dma((3,)), dma((3,)), dma((3,)), dma((3,)),
                dma((2, 4)), dma((2, 4)), dma((2,)), dma((2,)), dma((3,)), dma((3,)),
            ],
            compiler_params=pltpu.CompilerParams(
                collective_id=0, has_side_effects=True, vmem_limit_bytes=60 * 1024 * 1024),
        )(slide_planes, fields, melt_planes)

    return jax.shard_map(
        body, mesh=mesh,
        in_specs=(P(None, "grow", "wide", None), P(None, None, "wide", None), P()),
        out_specs=P(None, "grow", "wide", None), check_vma=False)
```

```python
import functools

import jax
import jax.numpy as jnp
from jax import lax
from jax.experimental import pallas as pl
from jax.experimental.pallas import tpu as pltpu
from jax.sharding import PartitionSpec as P

MESH = pl.DeviceIdType.MESH
STEPS = 8
OWN = 16
FAR = 8
PLANES = OWN + OWN + FAR
COLS = 32
LO = 16
ROWS = 64
PAD = 2
HALF = 8
QUAD = 4
RING = 4


def kernel(G, W, slide, fields, melt, out, lev, mbuf, rbuf, ebuf, cur, local_sem,
           n_send, n_recv, r_send, r_recv, f_send, f_recv, y_send, y_recv, m_send, m_recv, e_send, e_recv):
    g = lax.axis_index("grow")
    w = lax.axis_index("wide")
    base = OWN * (G - g)
    has_left, has_right = w > 0, w < W - 1
    start, place = g - g % RING, g % RING
    relay_to = start + (place + 1) % RING
    relay_from = start + (place + RING - 1) % RING
    source = g + 2
    far_from = source - source % RING + (source + 1) % RING
    relays = relay_from > 1
    partners = (
        (g > 0, {"grow": g - 1}), (g < G - 1, {"grow": g + 1}),
        (g > 1, {"grow": relay_to}), (relays, {"grow": relay_from}),
        (relays, {"grow": relay_from - 2}), (g < G - 2, {"grow": far_from}),
        (has_left, {"wide": w - 1}), (has_right, {"wide": w + 1}),
    )
    barrier = pltpu.get_barrier_semaphore()
    count = jnp.int32(0)
    for there, device in partners:
        count = count + there.astype(jnp.int32)

        @pl.when(there)
        def _():
            pl.semaphore_signal(barrier, inc=1, device_id=device, device_id_type=MESH)

    own = pltpu.make_async_copy(fields, lev.at[0, :, pl.ds(PAD + 0, OWN), pl.ds(LO, COLS), :], local_sem.at[0])
    own.start()
    melt_in = pltpu.make_async_copy(melt, mbuf.at[:, :, pl.ds(LO, COLS), :], local_sem.at[1])

    @pl.when(g >= G - 2)
    def _():
        melt_in.start()

    cursor = jnp.int32(0)
    cur[0] = cursor
    for k in range(STEPS):
        cursor = cursor + slide[k]
        cur[k + 1] = cursor

    zeros = jnp.zeros((8, 128), jnp.float32)
    for side_there, row in ((has_left, LO - 8), (has_right, LO + COLS)):

        @pl.when(jnp.logical_not(side_there))
        def _():
            @pl.loop(0, PLANES)
            def _(x):
                for f in range(3):
                    lev[0, f, PAD + x, pl.ds(row, 8), :] = zeros

            @pl.loop(0, OWN)
            def _(x):
                for f in range(3):
                    mbuf[f, x, pl.ds(row, 8), :] = zeros

    def zero_planes(first, last):
        @pl.loop(first, last)
        def _(x):
            for f in range(3):
                for k in range(6):
                    lev[0, f, PAD + x, pl.ds(LO - 8 + 8 * k, 8), :] = zeros

    @pl.when(g == G - 1)
    def _():
        zero_planes(OWN, PLANES)

    @pl.when(g == G - 2)
    def _():
        zero_planes(2 * OWN, PLANES)

    def remote(src, dst, sems, index, device):
        return pltpu.make_async_remote_copy(
            src_ref=src, dst_ref=dst, send_sem=sems[0].at[index], recv_sem=sems[1].at[index],
            device_id=device, device_id_type=MESH)

    def near(part):
        if part < 4:
            first, planes, row, rows = HALF * (part // 2), HALF, (COLS - 8) * (part % 2), 8
        else:
            first, planes, row, rows = QUAD * (part - 4), QUAD, 8, COLS - 16
        return remote(fields.at[:, pl.ds(first, planes), pl.ds(row, rows), :],
                      lev.at[0, :, pl.ds(PAD + OWN + first, planes), pl.ds(LO + row, rows), :],
                      (n_send, n_recv), part, {"grow": g - 1})

    far_rows = ((0, 8), (COLS - 8, 8), (8, COLS - 16))

    def relay(part):
        rows = pl.ds(*far_rows[part])
        return remote(fields.at[:, pl.ds(0, FAR), rows, :], rbuf.at[:, :, rows, :],
                      (r_send, r_recv), part, {"grow": relay_to})

    def far(part):
        row, rows = far_rows[part]
        return remote(rbuf.at[:, :, pl.ds(row, rows), :],
                      lev.at[0, :, pl.ds(PAD + 2 * OWN, FAR), pl.ds(LO + row, rows), :],
                      (f_send, f_recv), part, {"grow": relay_from - 2})

    middle = (w == W // 2 - 1, w == W // 2)
    in_middle = jnp.logical_or(*middle)

    def halo(first, planes, side):
        return lev.at[0, :, pl.ds(PAD + first, planes), pl.ds((LO + COLS, LO - 8)[side], 8), :]

    def near_halo(side, half):
        first = HALF * half
        return remote(halo(first, HALF, side), halo(OWN + first, HALF, side), (e_send, e_recv), 3 * half, {"grow": g - 1})

    def relay_halo(side):
        return remote(halo(0, FAR, side), ebuf, (e_send, e_recv), 1, {"grow": relay_to})

    def far_halo(side):
        return remote(ebuf, halo(2 * OWN, FAR, side), (e_send, e_recv), 2, {"grow": relay_from - 2})

    def y_own(side):
        rows, to, there = ((0, LO + COLS, w - 1), (COLS - 8, LO - 8, w + 1))[side]
        return pltpu.make_async_remote_copy(
            src_ref=fields.at[:, :, pl.ds(rows, 8), :],
            dst_ref=lev.at[0, :, pl.ds(PAD + 0, OWN), pl.ds(to, 8), :],
            send_sem=y_send.at[side, 3], recv_sem=y_recv.at[side, 3],
            device_id={"wide": there}, device_id_type=MESH)

    def y_melt(side):
        rows, to, there = ((0, LO + COLS, w - 1), (COLS - 8, LO - 8, w + 1))[side]
        return pltpu.make_async_remote_copy(
            src_ref=melt.at[:, :, pl.ds(rows, 8), :],
            dst_ref=mbuf.at[:, :, pl.ds(to, 8), :],
            send_sem=m_send.at[side], recv_sem=m_recv.at[side],
            device_id={"wide": there}, device_id_type=MESH)

    def y_copy(side, c):
        row, to, there = ((LO, LO + COLS, w - 1), (LO + COLS - 8, LO - 8, w + 1))[side]
        planes = pl.ds(PAD + OWN + HALF * c, HALF)
        return remote(lev.at[0, :, planes, pl.ds(row, 8), :], lev.at[0, :, planes, pl.ds(to, 8), :],
                      (y_send.at[side], y_recv.at[side]), c, {"wide": there})

    sends = (has_left, has_right)
    receives = (has_right, has_left)
    passes = (jnp.logical_and(has_left, w != W // 2), jnp.logical_and(has_right, w != W // 2 - 1))
    gets = (jnp.logical_and(has_right, w != W // 2 - 1), jnp.logical_and(has_left, w != W // 2))

    pl.semaphore_wait(barrier, count)
    for side in (0, 1):
        @pl.when(sends[side])
        def _():
            y_own(side).start()

    @pl.when(g > 0)
    def _():
        for part in range(6):
            near(part).start()

        @pl.when(jnp.logical_not(in_middle))
        def _():
            for part in range(6, 8):
                near(part).start()

    @pl.when(g > 1)
    def _():
        for part in range(3):
            relay(part).start()

    @pl.when(g >= G - 2)
    def _():
        for side in (0, 1):
            @pl.when(sends[side])
            def _():
                y_melt(side).start()

    def advance(t, x, n):
        for k in range(6):
            row = LO - 8 + 8 * k
            total, centre = [[] for _ in range(n)], [[] for _ in range(n)]
            for f in range(3):
                along = [lev[t, f, PAD + x + d, pl.ds(row, 8), :] for d in range(-1, n + 1)]
                for q in range(n):
                    here = along[q + 1]
                    around = along[q] + along[q + 2]
                    around = around + lev[t, f, PAD + x + q, pl.ds(row - 1, 8), :] + lev[t, f, PAD + x + q, pl.ds(row + 1, 8), :]
                    around = around + (pltpu.roll(here, 1, 1) + pltpu.roll(here, 127, 1))
                    total[q].append(around)
                    centre[q].append(here)
            for q in range(n):
                p, s, h = centre[q]
                p2 = p * p
                rest = 1.0 - p2
                drive = p * (0.4 - 0.3 * p2) + 0.15 * total[q][0] - rest * rest * (0.4 * h + 0.6 * s)
                grown = jnp.tanh(drive)
                change = 0.5 * (grown - p)
                s = (0.4 * s + 0.1 * total[q][1]) + change
                h = (0.04 * h + 0.16 * total[q][2]) + change
                new = [grown, s, h]
                if k == 0:
                    new = [jnp.where(has_left, v, 0.0) for v in new]
                if k == 5:
                    new = [jnp.where(has_right, v, 0.0) for v in new]
                for f in range(3):
                    lev[t + 1, f, PAD + x + q, pl.ds(row, 8), :] = new[f]

    span = pl.ds(LO - 8, COLS + 16)

    def left_edge(t, x, n):
        @pl.when(jnp.logical_and(g == 0, x < OWN))
        def _():
            for q in range(n):
                keep = x + q >= cur[t + 1]
                for f in range(3):
                    lev[t + 1, f, PAD + x + q, span, :] = jnp.where(keep, lev[t + 1, f, PAD + x + q, span, :], 0.0)

    def right_edge(t, x, n):
        @pl.when(x + n > base)
        def _():
            before, after = cur[t], cur[t + 1]
            for q in range(n):
                plane = x + q - base
                slot = jnp.clip(plane, 0, OWN - 1)
                inside = before > plane
                enters = after > plane
                for f in range(3):
                    fresh = jnp.where(enters, mbuf[f, slot, span, :], 0.0)
                    lev[t + 1, f, PAD + x + q, span, :] = jnp.where(inside, lev[t + 1, f, PAD + x + q, span, :], fresh)

    def pass_on(c, copies):
        for side in (0, 1):
            copies[side].wait_recv()

            @pl.when(passes[side])
            def _():
                y_copy(side, c).start()

    def near_edges(half):
        @pl.when(g < G - 1)
        def _():
            pass_on(half, (near(2 * half), near(2 * half + 1)))

    def far_edges():
        @pl.when(g < G - 2)
        def _():
            pass_on(2, (far(0), far(1)))

    def hand_over(*parts):
        @pl.when(relays)
        def _():
            for part in parts:
                relay(part).wait_recv()
                far(part).start()

    def edges_in(c):
        for side in (0, 1):
            @pl.when(gets[side])
            def _():
                y_copy(side, c).wait_recv()

    near_edges(0)
    hand_over(0, 1)
    near_edges(1)

    own.wait()
    for side in (0, 1):
        @pl.when(receives[side])
        def _():
            y_own(side).wait_recv()

    for side in (0, 1):
        @pl.when(jnp.logical_and(middle[side], g > 0))
        def _():
            near_halo(side, 0).start()
            near_halo(side, 1).start()
            for part in range(6, 8):
                near(part).start()

        @pl.when(jnp.logical_and(middle[side], g > 1))
        def _():
            relay_halo(side).start()

    @pl.when(in_middle)
    def _():
        hand_over(2)
        far_edges()

    @pl.when(g >= G - 2)
    def _():
        melt_in.wait()
        for side in (0, 1):
            @pl.when(receives[side])
            def _():
                y_melt(side).wait_recv()

    @pl.loop(0, STEPS - 1)
    def _(t):
        groups = (OWN - 2 - 2 * t + 3) // 4

        @pl.loop(0, groups)
        def _(i):
            x = OWN - 1 - t - 4 * (groups - i)
            advance(t, x, 4)
            left_edge(t, x, 4)

    @pl.when(jnp.logical_not(in_middle))
    def _():
        hand_over(2)

    for side in (0, 1):
        @pl.when(jnp.logical_and(middle[side], relays))
        def _():
            relay_halo(side).wait_recv()
            far_halo(side).start()

    @pl.loop(0, 5)
    def _(stage):
        for k in range(4):
            @pl.when(jnp.logical_and(stage == k, g < G - 1))
            def _():
                near(4 + k).wait_recv()
                if k % 2 == 0:
                    edges_in(k // 2)

        @pl.when(jnp.logical_and(stage == 0, jnp.logical_not(in_middle)))
        def _():
            far_edges()

        for side in (0, 1):
            for half in (0, 1):
                @pl.when(jnp.logical_and(jnp.logical_and(stage == 2 * half, g < G - 1), middle[side]))
                def _():
                    near_halo(side, half).wait_recv()

        @pl.when(jnp.logical_and(stage == 4, g < G - 2))
        def _():
            far(2).wait_recv()
            edges_in(2)
            for side in (0, 1):
                @pl.when(middle[side])
                def _():
                    far_halo(side).wait_recv()

        first = OWN + QUAD * stage
        parts = jnp.where(stage == 4, 2, 1)

        @pl.loop(0, STEPS)
        def _(t):
            @pl.loop(0, parts)
            def _(i):
                x = first - 1 - t + QUAD * i
                advance(t, x, QUAD)
                left_edge(t, x, QUAD)
                right_edge(t, x, QUAD)

    shift = cur[STEPS]
    @pl.loop(0, OWN)
    def _(x):
        for f in range(3):
            out[f, x] = lev[STEPS, f, PAD + shift + x, pl.ds(LO, COLS), :]

    for side in (0, 1):
        @pl.when(sends[side])
        def _():
            y_own(side).wait_send()

            @pl.when(g >= G - 2)
            def _():
                y_melt(side).wait_send()

        @pl.when(jnp.logical_and(passes[side], g < G - 1))
        def _():
            y_copy(side, 0).wait_send()
            y_copy(side, 1).wait_send()

        @pl.when(jnp.logical_and(passes[side], g < G - 2))
        def _():
            y_copy(side, 2).wait_send()

        @pl.when(jnp.logical_and(middle[side], g > 0))
        def _():
            near_halo(side, 0).wait_send()
            near_halo(side, 1).wait_send()

        @pl.when(jnp.logical_and(middle[side], g > 1))
        def _():
            relay_halo(side).wait_send()

        @pl.when(jnp.logical_and(middle[side], relays))
        def _():
            far_halo(side).wait_send()

    @pl.when(g > 0)
    def _():
        for part in range(8):
            near(part).wait_send()

    for part in range(3):
        @pl.when(g > 1)
        def _():
            relay(part).wait_send()

        @pl.when(relays)
        def _():
            far(part).wait_send()


def solution(mesh):
    G, W = mesh.shape["grow"], mesh.shape["wide"]

    def body(fields, melt_planes, slide_planes):
        dma = pltpu.SemaphoreType.DMA
        return pl.pallas_call(
            functools.partial(kernel, G, W),
            out_shape=jax.ShapeDtypeStruct(fields.shape, jnp.float32),
            in_specs=[
                pl.BlockSpec(memory_space=pltpu.SMEM),
                pl.BlockSpec(memory_space=pltpu.HBM),
                pl.BlockSpec(memory_space=pltpu.HBM),
            ],
            out_specs=pl.BlockSpec(memory_space=pltpu.VMEM),
            scratch_shapes=[
                pltpu.VMEM((STEPS + 1, 3, PAD + PLANES, ROWS, 128), jnp.float32),
                pltpu.VMEM((3, OWN, ROWS, 128), jnp.float32),
                pltpu.VMEM((3, FAR, COLS, 128), jnp.float32),
                pltpu.VMEM((3, FAR, 8, 128), jnp.float32),
                pltpu.SMEM((STEPS + 1,), jnp.int32),
                dma((2,)), dma((8,)), dma((8,)), dma((3,)), dma((3,)), dma((3,)), dma((3,)),
                dma((2, 4)), dma((2, 4)), dma((2,)), dma((2,)), dma((4,)), dma((4,)),
            ],
            compiler_params=pltpu.CompilerParams(
                collective_id=0, has_side_effects=True, vmem_limit_bytes=54000 * 1024),
        )(slide_planes, fields, melt_planes)

    return jax.shard_map(
        body, mesh=mesh,
        in_specs=(P(None, "grow", "wide", None), P(None, None, "wide", None), P()),
        out_specs=P(None, "grow", "wide", None), check_vma=False)
```

```python
import functools

import jax
import jax.numpy as jnp
from jax import lax
from jax.experimental import pallas as pl
from jax.experimental.pallas import tpu as pltpu
from jax.sharding import PartitionSpec as P

MESH = pl.DeviceIdType.MESH
STEPS = 8
OWN = 16
FAR = 8
PLANES = OWN + OWN + FAR
COLS = 32
LO = 16
ROWS = 64
PAD = 2
HALF = 8
QUAD = 4
RING = 4


def kernel(G, W, slide, fields, melt, out, lev, mbuf, rbuf, ebuf, cur, local_sem,
           n_send, n_recv, r_send, r_recv, f_send, f_recv, y_send, y_recv, m_send, m_recv, e_send, e_recv):
    g = lax.axis_index("grow")
    w = lax.axis_index("wide")
    base = OWN * (G - g)
    has_left, has_right = w > 0, w < W - 1
    start, place = g - g % RING, g % RING
    relay_to = start + (place + 1) % RING
    relay_from = start + (place + RING - 1) % RING
    source = g + 2
    far_from = source - source % RING + (source + 1) % RING
    relays = relay_from > 1
    partners = (
        (g > 0, {"grow": g - 1}), (g < G - 1, {"grow": g + 1}),
        (g > 1, {"grow": relay_to}), (relays, {"grow": relay_from}),
        (relays, {"grow": relay_from - 2}), (g < G - 2, {"grow": far_from}),
        (has_left, {"wide": w - 1}), (has_right, {"wide": w + 1}),
    )
    barrier = pltpu.get_barrier_semaphore()
    count = jnp.int32(0)
    for there, device in partners:
        count = count + there.astype(jnp.int32)

        @pl.when(there)
        def _():
            pl.semaphore_signal(barrier, inc=1, device_id=device, device_id_type=MESH)

    own = pltpu.make_async_copy(fields, lev.at[0, :, pl.ds(PAD + 0, OWN), pl.ds(LO, COLS), :], local_sem.at[0])
    own.start()
    melt_in = pltpu.make_async_copy(melt, mbuf.at[:, :, pl.ds(LO, COLS), :], local_sem.at[1])

    @pl.when(g >= G - 2)
    def _():
        melt_in.start()

    cursor = jnp.int32(0)
    cur[0] = cursor
    for k in range(STEPS):
        cursor = cursor + slide[k]
        cur[k + 1] = cursor

    zeros = jnp.zeros((8, 128), jnp.float32)
    for side_there, row in ((has_left, LO - 8), (has_right, LO + COLS)):

        @pl.when(jnp.logical_not(side_there))
        def _():
            @pl.loop(0, PLANES)
            def _(x):
                for f in range(3):
                    lev[0, f, PAD + x, pl.ds(row, 8), :] = zeros

            @pl.loop(0, OWN)
            def _(x):
                for f in range(3):
                    mbuf[f, x, pl.ds(row, 8), :] = zeros

    def zero_planes(first, last):
        @pl.loop(first, last)
        def _(x):
            for f in range(3):
                for k in range(6):
                    lev[0, f, PAD + x, pl.ds(LO - 8 + 8 * k, 8), :] = zeros

    @pl.when(g == G - 1)
    def _():
        zero_planes(OWN, PLANES)

    @pl.when(g == G - 2)
    def _():
        zero_planes(2 * OWN, PLANES)

    def remote(src, dst, sems, index, device):
        return pltpu.make_async_remote_copy(
            src_ref=src, dst_ref=dst, send_sem=sems[0].at[index], recv_sem=sems[1].at[index],
            device_id=device, device_id_type=MESH)

    def near(part):
        if part < 4:
            first, planes, row, rows = HALF * (part // 2), HALF, (COLS - 8) * (part % 2), 8
        else:
            first, planes, row, rows = QUAD * (part - 4), QUAD, 8, COLS - 16
        return remote(fields.at[:, pl.ds(first, planes), pl.ds(row, rows), :],
                      lev.at[0, :, pl.ds(PAD + OWN + first, planes), pl.ds(LO + row, rows), :],
                      (n_send, n_recv), part, {"grow": g - 1})

    far_rows = ((0, 8), (COLS - 8, 8), (8, COLS - 16))

    def relay(part):
        rows = pl.ds(*far_rows[part])
        return remote(fields.at[:, pl.ds(0, FAR), rows, :], rbuf.at[:, :, rows, :],
                      (r_send, r_recv), part, {"grow": relay_to})

    def far(part):
        row, rows = far_rows[part]
        return remote(rbuf.at[:, :, pl.ds(row, rows), :],
                      lev.at[0, :, pl.ds(PAD + 2 * OWN, FAR), pl.ds(LO + row, rows), :],
                      (f_send, f_recv), part, {"grow": relay_from - 2})

    middle = (w == W // 2 - 1, w == W // 2)
    in_middle = jnp.logical_or(*middle)

    def halo(first, planes, side):
        return lev.at[0, :, pl.ds(PAD + first, planes), pl.ds((LO + COLS, LO - 8)[side], 8), :]

    def near_halo(side, half):
        first = HALF * half
        return remote(halo(first, HALF, side), halo(OWN + first, HALF, side), (e_send, e_recv), 3 * half, {"grow": g - 1})

    def relay_halo(side):
        return remote(halo(0, FAR, side), ebuf, (e_send, e_recv), 1, {"grow": relay_to})

    def far_halo(side):
        return remote(ebuf, halo(2 * OWN, FAR, side), (e_send, e_recv), 2, {"grow": relay_from - 2})

    def y_own(side):
        rows, to, there = ((0, LO + COLS, w - 1), (COLS - 8, LO - 8, w + 1))[side]
        return pltpu.make_async_remote_copy(
            src_ref=fields.at[:, :, pl.ds(rows, 8), :],
            dst_ref=lev.at[0, :, pl.ds(PAD + 0, OWN), pl.ds(to, 8), :],
            send_sem=y_send.at[side, 3], recv_sem=y_recv.at[side, 3],
            device_id={"wide": there}, device_id_type=MESH)

    def y_melt(side):
        rows, to, there = ((0, LO + COLS, w - 1), (COLS - 8, LO - 8, w + 1))[side]
        return pltpu.make_async_remote_copy(
            src_ref=melt.at[:, :, pl.ds(rows, 8), :],
            dst_ref=mbuf.at[:, :, pl.ds(to, 8), :],
            send_sem=m_send.at[side], recv_sem=m_recv.at[side],
            device_id={"wide": there}, device_id_type=MESH)

    def y_copy(side, c):
        row, to, there = ((LO, LO + COLS, w - 1), (LO + COLS - 8, LO - 8, w + 1))[side]
        planes = pl.ds(PAD + OWN + HALF * c, HALF)
        return remote(lev.at[0, :, planes, pl.ds(row, 8), :], lev.at[0, :, planes, pl.ds(to, 8), :],
                      (y_send.at[side], y_recv.at[side]), c, {"wide": there})

    sends = (has_left, has_right)
    receives = (has_right, has_left)
    passes = (jnp.logical_and(has_left, w != W // 2), jnp.logical_and(has_right, w != W // 2 - 1))
    gets = (jnp.logical_and(has_right, w != W // 2 - 1), jnp.logical_and(has_left, w != W // 2))

    pl.semaphore_wait(barrier, count)
    for side in (0, 1):
        @pl.when(sends[side])
        def _():
            y_own(side).start()

    @pl.when(g > 0)
    def _():
        for part in range(6):
            near(part).start()

        @pl.when(jnp.logical_not(in_middle))
        def _():
            for part in range(6, 8):
                near(part).start()

    @pl.when(g > 1)
    def _():
        for part in range(3):
            relay(part).start()

    @pl.when(g >= G - 2)
    def _():
        for side in (0, 1):
            @pl.when(sends[side])
            def _():
                y_melt(side).start()

    def advance(t, x, n):
        for k in range(6):
            row = LO - 8 + 8 * k
            total, centre = [[] for _ in range(n)], [[] for _ in range(n)]
            for f in range(3):
                along = [lev[t, f, PAD + x + d, pl.ds(row, 8), :] for d in range(-1, n + 1)]
                for q in range(n):
                    here = along[q + 1]
                    around = along[q] + along[q + 2]
                    around = around + lev[t, f, PAD + x + q, pl.ds(row - 1, 8), :] + lev[t, f, PAD + x + q, pl.ds(row + 1, 8), :]
                    around = around + (pltpu.roll(here, 1, 1) + pltpu.roll(here, 127, 1))
                    total[q].append(around)
                    centre[q].append(here)
            for q in range(n):
                p, s, h = centre[q]
                p2 = p * p
                rest = 1.0 - p2
                drive = p * (0.4 - 0.3 * p2) + 0.15 * total[q][0] - rest * rest * (0.4 * h + 0.6 * s)
                grown = jnp.tanh(drive)
                change = 0.5 * (grown - p)
                s = (0.4 * s + 0.1 * total[q][1]) + change
                h = (0.04 * h + 0.16 * total[q][2]) + change
                new = [grown, s, h]
                if k == 0:
                    new = [jnp.where(has_left, v, 0.0) for v in new]
                if k == 5:
                    new = [jnp.where(has_right, v, 0.0) for v in new]
                for f in range(3):
                    lev[t + 1, f, PAD + x + q, pl.ds(row, 8), :] = new[f]

    span = pl.ds(LO - 8, COLS + 16)

    def left_edge(t, x, n):
        reach = jnp.where(t == 0, -OWN, jnp.where(t < 3, OWN // 2, OWN))

        @pl.when(jnp.logical_and(g == 0, x < reach))
        def _():
            for q in range(n):
                keep = x + q >= cur[t + 1]
                for f in range(3):
                    lev[t + 1, f, PAD + x + q, span, :] = jnp.where(keep, lev[t + 1, f, PAD + x + q, span, :], 0.0)

    def right_edge(t, x, n):
        @pl.when(x + n > base)
        def _():
            before, after = cur[t], cur[t + 1]
            for q in range(n):
                plane = x + q - base
                slot = jnp.clip(plane, 0, OWN - 1)
                inside = before > plane
                enters = after > plane
                for f in range(3):
                    fresh = jnp.where(enters, mbuf[f, slot, span, :], 0.0)
                    lev[t + 1, f, PAD + x + q, span, :] = jnp.where(inside, lev[t + 1, f, PAD + x + q, span, :], fresh)

    def pass_on(c, copies):
        for side in (0, 1):
            copies[side].wait_recv()

            @pl.when(passes[side])
            def _():
                y_copy(side, c).start()

    def near_edges(half):
        @pl.when(g < G - 1)
        def _():
            pass_on(half, (near(2 * half), near(2 * half + 1)))

    def far_edges():
        @pl.when(g < G - 2)
        def _():
            pass_on(2, (far(0), far(1)))

    def hand_over(*parts):
        @pl.when(relays)
        def _():
            for part in parts:
                relay(part).wait_recv()
                far(part).start()

    def edges_in(c):
        for side in (0, 1):
            @pl.when(gets[side])
            def _():
                y_copy(side, c).wait_recv()

    near_edges(0)
    hand_over(0, 1)
    near_edges(1)

    own.wait()
    for side in (0, 1):
        @pl.when(receives[side])
        def _():
            y_own(side).wait_recv()

    for side in (0, 1):
        @pl.when(jnp.logical_and(middle[side], g > 0))
        def _():
            near_halo(side, 0).start()
            near_halo(side, 1).start()
            for part in range(6, 8):
                near(part).start()

        @pl.when(jnp.logical_and(middle[side], g > 1))
        def _():
            relay_halo(side).start()

    @pl.when(in_middle)
    def _():
        hand_over(2)
        far_edges()

    @pl.when(g >= G - 2)
    def _():
        melt_in.wait()
        for side in (0, 1):
            @pl.when(receives[side])
            def _():
                y_melt(side).wait_recv()

    @pl.loop(0, STEPS - 1)
    def _(t):
        groups = (OWN - 2 - 2 * t + 3) // 4

        @pl.loop(0, groups)
        def _(i):
            x = OWN - 1 - t - 4 * (groups - i)
            advance(t, x, 4)
            left_edge(t, x, 4)

    @pl.when(jnp.logical_not(in_middle))
    def _():
        hand_over(2)

    for side in (0, 1):
        @pl.when(jnp.logical_and(middle[side], relays))
        def _():
            relay_halo(side).wait_recv()
            far_halo(side).start()

    @pl.loop(0, 5)
    def _(stage):
        for k in range(4):
            @pl.when(jnp.logical_and(stage == k, g < G - 1))
            def _():
                near(4 + k).wait_recv()
                if k % 2 == 0:
                    edges_in(k // 2)

        @pl.when(jnp.logical_and(stage == 0, jnp.logical_not(in_middle)))
        def _():
            far_edges()

        for side in (0, 1):
            for half in (0, 1):
                @pl.when(jnp.logical_and(jnp.logical_and(stage == 2 * half, g < G - 1), middle[side]))
                def _():
                    near_halo(side, half).wait_recv()

        @pl.when(jnp.logical_and(stage == 4, g < G - 2))
        def _():
            far(2).wait_recv()
            edges_in(2)
            for side in (0, 1):
                @pl.when(middle[side])
                def _():
                    far_halo(side).wait_recv()

        first = OWN + QUAD * stage
        parts = jnp.where(stage == 4, 2, 1)

        @pl.loop(0, STEPS)
        def _(t):
            @pl.loop(0, parts)
            def _(i):
                x = first - 1 - t + QUAD * i
                advance(t, x, QUAD)
                left_edge(t, x, QUAD)
                right_edge(t, x, QUAD)

    shift = cur[STEPS]
    @pl.loop(0, OWN)
    def _(x):
        for f in range(3):
            out[f, x] = lev[STEPS, f, PAD + shift + x, pl.ds(LO, COLS), :]

    for side in (0, 1):
        @pl.when(sends[side])
        def _():
            y_own(side).wait_send()

            @pl.when(g >= G - 2)
            def _():
                y_melt(side).wait_send()

        @pl.when(jnp.logical_and(passes[side], g < G - 1))
        def _():
            y_copy(side, 0).wait_send()
            y_copy(side, 1).wait_send()

        @pl.when(jnp.logical_and(passes[side], g < G - 2))
        def _():
            y_copy(side, 2).wait_send()

        @pl.when(jnp.logical_and(middle[side], g > 0))
        def _():
            near_halo(side, 0).wait_send()
            near_halo(side, 1).wait_send()

        @pl.when(jnp.logical_and(middle[side], g > 1))
        def _():
            relay_halo(side).wait_send()

        @pl.when(jnp.logical_and(middle[side], relays))
        def _():
            far_halo(side).wait_send()

    @pl.when(g > 0)
    def _():
        for part in range(8):
            near(part).wait_send()

    for part in range(3):
        @pl.when(g > 1)
        def _():
            relay(part).wait_send()

        @pl.when(relays)
        def _():
            far(part).wait_send()


def solution(mesh):
    G, W = mesh.shape["grow"], mesh.shape["wide"]

    def body(fields, melt_planes, slide_planes):
        dma = pltpu.SemaphoreType.DMA
        return pl.pallas_call(
            functools.partial(kernel, G, W),
            out_shape=jax.ShapeDtypeStruct(fields.shape, jnp.float32),
            in_specs=[
                pl.BlockSpec(memory_space=pltpu.SMEM),
                pl.BlockSpec(memory_space=pltpu.HBM),
                pl.BlockSpec(memory_space=pltpu.HBM),
            ],
            out_specs=pl.BlockSpec(memory_space=pltpu.VMEM),
            scratch_shapes=[
                pltpu.VMEM((STEPS + 1, 3, PAD + PLANES, ROWS, 128), jnp.float32),
                pltpu.VMEM((3, OWN, ROWS, 128), jnp.float32),
                pltpu.VMEM((3, FAR, COLS, 128), jnp.float32),
                pltpu.VMEM((3, FAR, 8, 128), jnp.float32),
                pltpu.SMEM((STEPS + 1,), jnp.int32),
                dma((2,)), dma((8,)), dma((8,)), dma((3,)), dma((3,)), dma((3,)), dma((3,)),
                dma((2, 4)), dma((2, 4)), dma((2,)), dma((2,)), dma((4,)), dma((4,)),
            ],
            compiler_params=pltpu.CompilerParams(
                collective_id=0, has_side_effects=True, vmem_limit_bytes=54000 * 1024),
        )(slide_planes, fields, melt_planes)

    return jax.shard_map(
        body, mesh=mesh,
        in_specs=(P(None, "grow", "wide", None), P(None, None, "wide", None), P()),
        out_specs=P(None, "grow", "wide", None), check_vma=False)
```

```python
import functools

import jax
import jax.numpy as jnp
from jax import lax
from jax.experimental import pallas as pl
from jax.experimental.pallas import tpu as pltpu
from jax.sharding import PartitionSpec as P

MESH = pl.DeviceIdType.MESH
STEPS = 8
OWN = 16
FAR = 8
PLANES = OWN + OWN + FAR
COLS = 32
LO = 16
ROWS = 64
PAD = 2
HALF = 8
QUAD = 4
RING = 4


def kernel(G, W, slide, fields, melt, out, lev, mbuf, rbuf, ebuf, cur, local_sem,
           n_send, n_recv, r_send, r_recv, f_send, f_recv, y_send, y_recv, m_send, m_recv, e_send, e_recv):
    g = lax.axis_index("grow")
    w = lax.axis_index("wide")
    base = OWN * (G - g)
    has_left, has_right = w > 0, w < W - 1
    start, place = g - g % RING, g % RING
    relay_to = start + (place + 1) % RING
    relay_from = start + (place + RING - 1) % RING
    source = g + 2
    far_from = source - source % RING + (source + 1) % RING
    relays = relay_from > 1
    partners = (
        (g > 0, {"grow": g - 1}), (g < G - 1, {"grow": g + 1}),
        (g > 1, {"grow": relay_to}), (relays, {"grow": relay_from}),
        (relays, {"grow": relay_from - 2}), (g < G - 2, {"grow": far_from}),
        (has_left, {"wide": w - 1}), (has_right, {"wide": w + 1}),
    )
    barrier = pltpu.get_barrier_semaphore()
    count = jnp.int32(0)
    for there, device in partners:
        count = count + there.astype(jnp.int32)

        @pl.when(there)
        def _():
            pl.semaphore_signal(barrier, inc=1, device_id=device, device_id_type=MESH)

    own = pltpu.make_async_copy(fields, lev.at[0, :, pl.ds(PAD + 0, OWN), pl.ds(LO, COLS), :], local_sem.at[0])
    own.start()
    melt_in = pltpu.make_async_copy(melt, mbuf.at[:, :, pl.ds(LO, COLS), :], local_sem.at[1])

    @pl.when(g >= G - 2)
    def _():
        melt_in.start()

    cursor = jnp.int32(0)
    cur[0] = cursor
    for k in range(STEPS):
        cursor = cursor + slide[k]
        cur[k + 1] = cursor

    zeros = jnp.zeros((8, 128), jnp.float32)
    for side_there, row in ((has_left, LO - 8), (has_right, LO + COLS)):

        @pl.when(jnp.logical_not(side_there))
        def _():
            @pl.loop(0, PLANES)
            def _(x):
                for f in range(3):
                    lev[0, f, PAD + x, pl.ds(row, 8), :] = zeros

            @pl.loop(0, OWN)
            def _(x):
                for f in range(3):
                    mbuf[f, x, pl.ds(row, 8), :] = zeros

    def zero_planes(first, last):
        @pl.loop(first, last)
        def _(x):
            for f in range(3):
                for k in range(6):
                    lev[0, f, PAD + x, pl.ds(LO - 8 + 8 * k, 8), :] = zeros

    @pl.when(g == G - 1)
    def _():
        zero_planes(OWN, PLANES)

    @pl.when(g == G - 2)
    def _():
        zero_planes(2 * OWN, PLANES)

    def remote(src, dst, sems, index, device):
        return pltpu.make_async_remote_copy(
            src_ref=src, dst_ref=dst, send_sem=sems[0].at[index], recv_sem=sems[1].at[index],
            device_id=device, device_id_type=MESH)

    def near(part):
        if part < 4:
            first, planes, row, rows = HALF * (part // 2), HALF, (COLS - 8) * (part % 2), 8
        else:
            first, planes, row, rows = QUAD * (part - 4), QUAD, 8, COLS - 16
        return remote(fields.at[:, pl.ds(first, planes), pl.ds(row, rows), :],
                      lev.at[0, :, pl.ds(PAD + OWN + first, planes), pl.ds(LO + row, rows), :],
                      (n_send, n_recv), part, {"grow": g - 1})

    far_rows = ((0, 8), (COLS - 8, 8), (8, COLS - 16))

    def relay(part):
        rows = pl.ds(*far_rows[part])
        return remote(fields.at[:, pl.ds(0, FAR), rows, :], rbuf.at[:, :, rows, :],
                      (r_send, r_recv), part, {"grow": relay_to})

    def far(part):
        row, rows = far_rows[part]
        return remote(rbuf.at[:, :, pl.ds(row, rows), :],
                      lev.at[0, :, pl.ds(PAD + 2 * OWN, FAR), pl.ds(LO + row, rows), :],
                      (f_send, f_recv), part, {"grow": relay_from - 2})

    middle = (w == W // 2 - 1, w == W // 2)
    in_middle = jnp.logical_or(*middle)

    def halo(first, planes, side):
        return lev.at[0, :, pl.ds(PAD + first, planes), pl.ds((LO + COLS, LO - 8)[side], 8), :]

    def near_halo(side, half):
        first = HALF * half
        return remote(halo(first, HALF, side), halo(OWN + first, HALF, side), (e_send, e_recv), 3 * half, {"grow": g - 1})

    def relay_halo(side):
        return remote(halo(0, FAR, side), ebuf, (e_send, e_recv), 1, {"grow": relay_to})

    def far_halo(side):
        return remote(ebuf, halo(2 * OWN, FAR, side), (e_send, e_recv), 2, {"grow": relay_from - 2})

    def y_own(side):
        rows, to, there = ((0, LO + COLS, w - 1), (COLS - 8, LO - 8, w + 1))[side]
        return pltpu.make_async_remote_copy(
            src_ref=fields.at[:, :, pl.ds(rows, 8), :],
            dst_ref=lev.at[0, :, pl.ds(PAD + 0, OWN), pl.ds(to, 8), :],
            send_sem=y_send.at[side, 3], recv_sem=y_recv.at[side, 3],
            device_id={"wide": there}, device_id_type=MESH)

    def y_melt(side):
        rows, to, there = ((0, LO + COLS, w - 1), (COLS - 8, LO - 8, w + 1))[side]
        return pltpu.make_async_remote_copy(
            src_ref=melt.at[:, :, pl.ds(rows, 8), :],
            dst_ref=mbuf.at[:, :, pl.ds(to, 8), :],
            send_sem=m_send.at[side], recv_sem=m_recv.at[side],
            device_id={"wide": there}, device_id_type=MESH)

    def y_copy(side, c):
        row, to, there = ((LO, LO + COLS, w - 1), (LO + COLS - 8, LO - 8, w + 1))[side]
        planes = pl.ds(PAD + OWN + HALF * c, HALF)
        return remote(lev.at[0, :, planes, pl.ds(row, 8), :], lev.at[0, :, planes, pl.ds(to, 8), :],
                      (y_send.at[side], y_recv.at[side]), c, {"wide": there})

    sends = (has_left, has_right)
    receives = (has_right, has_left)
    passes = (jnp.logical_and(has_left, w != W // 2), jnp.logical_and(has_right, w != W // 2 - 1))
    gets = (jnp.logical_and(has_right, w != W // 2 - 1), jnp.logical_and(has_left, w != W // 2))

    pl.semaphore_wait(barrier, count)
    for side in (0, 1):
        @pl.when(middle[1 - side])
        def _():
            y_own(side).start()

    for side in (0, 1):
        @pl.when(passes[side])
        def _():
            y_own(side).start()

    @pl.when(g > 0)
    def _():
        for part in range(6):
            near(part).start()

        @pl.when(jnp.logical_not(in_middle))
        def _():
            for part in range(6, 8):
                near(part).start()

    @pl.when(g > 1)
    def _():
        for part in range(3):
            relay(part).start()

    @pl.when(g >= G - 2)
    def _():
        for side in (0, 1):
            @pl.when(sends[side])
            def _():
                y_melt(side).start()

    def advance(t, x, n):
        for k in range(6):
            row = LO - 8 + 8 * k
            total, centre = [[] for _ in range(n)], [[] for _ in range(n)]
            for f in range(3):
                along = [lev[t, f, PAD + x + d, pl.ds(row, 8), :] for d in range(-1, n + 1)]
                for q in range(n):
                    here = along[q + 1]
                    around = along[q] + along[q + 2]
                    around = around + lev[t, f, PAD + x + q, pl.ds(row - 1, 8), :] + lev[t, f, PAD + x + q, pl.ds(row + 1, 8), :]
                    around = around + (pltpu.roll(here, 1, 1) + pltpu.roll(here, 127, 1))
                    total[q].append(around)
                    centre[q].append(here)
            for q in range(n):
                p, s, h = centre[q]
                p2 = p * p
                rest = 1.0 - p2
                drive = p * (0.4 - 0.3 * p2) + 0.15 * total[q][0] - rest * rest * (0.4 * h + 0.6 * s)
                grown = jnp.tanh(drive)
                change = 0.5 * (grown - p)
                s = (0.4 * s + 0.1 * total[q][1]) + change
                h = (0.04 * h + 0.16 * total[q][2]) + change
                new = [grown, s, h]
                if k == 0:
                    new = [jnp.where(has_left, v, 0.0) for v in new]
                if k == 5:
                    new = [jnp.where(has_right, v, 0.0) for v in new]
                for f in range(3):
                    lev[t + 1, f, PAD + x + q, pl.ds(row, 8), :] = new[f]

    span = pl.ds(LO - 8, COLS + 16)

    def left_edge(t, x, n):
        reach = jnp.where(t == 0, -OWN, jnp.where(t < 3, OWN // 2, OWN))

        @pl.when(jnp.logical_and(g == 0, x < reach))
        def _():
            for q in range(n):
                keep = x + q >= cur[t + 1]
                for f in range(3):
                    lev[t + 1, f, PAD + x + q, span, :] = jnp.where(keep, lev[t + 1, f, PAD + x + q, span, :], 0.0)

    def right_edge(t, x, n):
        @pl.when(x + n > base)
        def _():
            before, after = cur[t], cur[t + 1]
            for q in range(n):
                plane = x + q - base
                slot = jnp.clip(plane, 0, OWN - 1)
                inside = before > plane
                enters = after > plane
                for f in range(3):
                    fresh = jnp.where(enters, mbuf[f, slot, span, :], 0.0)
                    lev[t + 1, f, PAD + x + q, span, :] = jnp.where(inside, lev[t + 1, f, PAD + x + q, span, :], fresh)

    def pass_on(c, copies):
        for side in (0, 1):
            copies[side].wait_recv()

            @pl.when(passes[side])
            def _():
                y_copy(side, c).start()

    def near_edges(half):
        @pl.when(g < G - 1)
        def _():
            pass_on(half, (near(2 * half), near(2 * half + 1)))

    def far_edges():
        @pl.when(g < G - 2)
        def _():
            pass_on(2, (far(0), far(1)))

    def hand_over(*parts):
        @pl.when(relays)
        def _():
            for part in parts:
                relay(part).wait_recv()
                far(part).start()

    def edges_in(c):
        for side in (0, 1):
            @pl.when(gets[side])
            def _():
                y_copy(side, c).wait_recv()

    near_edges(0)
    hand_over(0, 1)
    near_edges(1)

    own.wait()
    for side in (0, 1):
        @pl.when(receives[side])
        def _():
            y_own(side).wait_recv()

    for side in (0, 1):
        @pl.when(jnp.logical_and(middle[side], g > 0))
        def _():
            near_halo(side, 0).start()
            near_halo(side, 1).start()
            for part in range(6, 8):
                near(part).start()

        @pl.when(jnp.logical_and(middle[side], g > 1))
        def _():
            relay_halo(side).start()

    @pl.when(in_middle)
    def _():
        hand_over(2)
        far_edges()

    @pl.when(g >= G - 2)
    def _():
        melt_in.wait()
        for side in (0, 1):
            @pl.when(receives[side])
            def _():
                y_melt(side).wait_recv()

    @pl.loop(0, STEPS - 1)
    def _(t):
        groups = (OWN - 2 - 2 * t + 3) // 4

        @pl.loop(0, groups)
        def _(i):
            x = OWN - 1 - t - 4 * (groups - i)
            advance(t, x, 4)
            left_edge(t, x, 4)

    @pl.when(jnp.logical_not(in_middle))
    def _():
        hand_over(2)

    for side in (0, 1):
        @pl.when(jnp.logical_and(middle[side], relays))
        def _():
            relay_halo(side).wait_recv()
            far_halo(side).start()

    @pl.loop(0, 5)
    def _(stage):
        for k in range(4):
            @pl.when(jnp.logical_and(stage == k, g < G - 1))
            def _():
                near(4 + k).wait_recv()
                if k % 2 == 0:
                    edges_in(k // 2)

        @pl.when(jnp.logical_and(stage == 0, jnp.logical_not(in_middle)))
        def _():
            far_edges()

        for side in (0, 1):
            for half in (0, 1):
                @pl.when(jnp.logical_and(jnp.logical_and(stage == 2 * half, g < G - 1), middle[side]))
                def _():
                    near_halo(side, half).wait_recv()

        @pl.when(jnp.logical_and(stage == 4, g < G - 2))
        def _():
            far(2).wait_recv()
            edges_in(2)
            for side in (0, 1):
                @pl.when(middle[side])
                def _():
                    far_halo(side).wait_recv()

        first = OWN + QUAD * stage
        parts = jnp.where(stage == 4, 2, 1)

        @pl.loop(0, STEPS)
        def _(t):
            @pl.loop(0, parts)
            def _(i):
                x = first - 1 - t + QUAD * i
                advance(t, x, QUAD)
                left_edge(t, x, QUAD)
                right_edge(t, x, QUAD)

    shift = cur[STEPS]
    @pl.loop(0, OWN)
    def _(x):
        for f in range(3):
            out[f, x] = lev[STEPS, f, PAD + shift + x, pl.ds(LO, COLS), :]

    for side in (0, 1):
        @pl.when(sends[side])
        def _():
            y_own(side).wait_send()

            @pl.when(g >= G - 2)
            def _():
                y_melt(side).wait_send()

        @pl.when(jnp.logical_and(passes[side], g < G - 1))
        def _():
            y_copy(side, 0).wait_send()
            y_copy(side, 1).wait_send()

        @pl.when(jnp.logical_and(passes[side], g < G - 2))
        def _():
            y_copy(side, 2).wait_send()

        @pl.when(jnp.logical_and(middle[side], g > 0))
        def _():
            near_halo(side, 0).wait_send()
            near_halo(side, 1).wait_send()

        @pl.when(jnp.logical_and(middle[side], g > 1))
        def _():
            relay_halo(side).wait_send()

        @pl.when(jnp.logical_and(middle[side], relays))
        def _():
            far_halo(side).wait_send()

    @pl.when(g > 0)
    def _():
        for part in range(8):
            near(part).wait_send()

    for part in range(3):
        @pl.when(g > 1)
        def _():
            relay(part).wait_send()

        @pl.when(relays)
        def _():
            far(part).wait_send()


def solution(mesh):
    G, W = mesh.shape["grow"], mesh.shape["wide"]

    def body(fields, melt_planes, slide_planes):
        dma = pltpu.SemaphoreType.DMA
        return pl.pallas_call(
            functools.partial(kernel, G, W),
            out_shape=jax.ShapeDtypeStruct(fields.shape, jnp.float32),
            in_specs=[
                pl.BlockSpec(memory_space=pltpu.SMEM),
                pl.BlockSpec(memory_space=pltpu.HBM),
                pl.BlockSpec(memory_space=pltpu.HBM),
            ],
            out_specs=pl.BlockSpec(memory_space=pltpu.VMEM),
            scratch_shapes=[
                pltpu.VMEM((STEPS + 1, 3, PAD + PLANES, ROWS, 128), jnp.float32),
                pltpu.VMEM((3, OWN, ROWS, 128), jnp.float32),
                pltpu.VMEM((3, FAR, COLS, 128), jnp.float32),
                pltpu.VMEM((3, FAR, 8, 128), jnp.float32),
                pltpu.SMEM((STEPS + 1,), jnp.int32),
                dma((2,)), dma((8,)), dma((8,)), dma((3,)), dma((3,)), dma((3,)), dma((3,)),
                dma((2, 4)), dma((2, 4)), dma((2,)), dma((2,)), dma((4,)), dma((4,)),
            ],
            compiler_params=pltpu.CompilerParams(
                collective_id=0, has_side_effects=True, vmem_limit_bytes=54000 * 1024),
        )(slide_planes, fields, melt_planes)

    return jax.shard_map(
        body, mesh=mesh,
        in_specs=(P(None, "grow", "wide", None), P(None, None, "wide", None), P()),
        out_specs=P(None, "grow", "wide", None), check_vma=False)
```
